512 devices in a mesh: dp: 8 (over z_hi, y), expert: 64 (over z_lo, x, core).
Axes of the slice: x: 4, y: 4, z: 16 (z_hi: 2, z_lo: 8; z = z_hi * 8 + z_lo), core: 2. Of those that a mesh axis runs over, the one named last changes fastest.
Arguments:
- hidden_rows: bfloat16 [768, 65536], P(None, ('dp', 'expert')), may hold values from -6 to 6
- grad_rows: bfloat16 [65536, 2560], P(('dp', 'expert')), may hold values from -0.1796875 to 0.1796875
- block_slot: int32 [512, 1], P(('dp', 'expert')), may hold values from 0 to 1
- live_rows: int32 [512], P(('dp', 'expert')), may hold values from 16 to 128
- replica_plan: int32 [64], replicated, may hold values from 0 to 15
- master: float32 [64, 768, 640], P('expert', 'dp'), may hold values from -0.21875 to 0.21875
- moment_one: float32 [64, 768, 640], P('expert', 'dp'), may hold values from -1.8 to 1.8
- moment_two: float32 [64, 768, 640], P('expert', 'dp'), may hold values from 0.01 to 1
Outputs:
- master_new: float32 [64, 768, 640], P('expert', 'dp')
- first_new: float32 [64, 768, 640], P('expert', 'dp')
- second_new: float32 [64, 768, 640], P('expert', 'dp')
- replica_weight: bfloat16 [64, 768, 2560], P('expert', 'dp')
The draws below stay inside these ranges and needn't reach their ends.
Inputs may be any that keep to these rules, and one draw needn't show every extreme that they name: replica_plan[j] is the expert of which the devices at index j along the expert axis host a replica; it may equal j mod 16. `block_slot`: 0 marks a block of the primary expert, 1 a block of the replica.
All inputs are finite; a program needn't handle non-finite values.
Results may differ from the reference program's by a relative error of at most 0.001.
Values may be sent and summed in bfloat16 or wider, within the bound.
A program may use at most 64 MiB of HBM per device.

```python
import math
import jax
import jax.numpy as jnp
import numpy as np
from jax import lax

D = 2560
HID = 768
QUART = 4
BLK = 128
BLOCKS = 1
ROWS = 128
EXPERTS = 16
N_DP = 8
N_EXPERT = 64


def with_ends(drawn, key, smallest, largest):
    longest = drawn.shape.index(max(drawn.shape))
    spots = []
    for shift in (0, 1):
        where = [jax.random.randint(jax.random.fold_in(key, axis), (), 0, length) for axis, length in enumerate(drawn.shape)]
        where[longest] = (where[longest] + shift) % drawn.shape[longest]
        spots.append(tuple(where))
    return drawn.at[spots[0]].set(smallest).at[spots[1]].set(largest)


def steps_of(key, dims, cuts, smallest, top_value):
    gain, own = 1.0, jax.random.fold_in(key, 6)
    for axis_at, blocks in cuts:
        draws = jnp.exp(jax.random.uniform(jax.random.fold_in(own, axis_at), (blocks,), jnp.float32, smallest / len(cuts), top_value / len(cuts)))
        gain = gain * jnp.repeat(draws, dims[axis_at] // blocks).reshape([-1 if axis == axis_at else 1 for axis in range(len(dims))])
    return gain


def rank_bounds(count, slope):
    loads = [(1 << 20) // math.isqrt(standing ** slope) + 1 for standing in range(1, count + 1)]
    scale = 1 + sum(loads) // (1 << 30)
    return np.cumsum(np.array([max(1, weight // scale) for weight in loads]))


def ranked(stream_key, dims, amount, slope):
    grid = rank_bounds(amount, slope)
    lot = jax.random.randint(jax.random.fold_in(stream_key, 1), dims, 0, int(grid[amount - 1]))
    rank = jnp.searchsorted(jnp.asarray(grid, jnp.int32), lot, side="right")
    return jax.random.permutation(jax.random.fold_in(stream_key, 2), amount)[rank].astype(jnp.int32)


def centred(key, dims, spread, bound, shards=(), dtype=jnp.bfloat16):
    result = jax.random.normal(key, dims, jnp.float32) * spread
    if len(shards) > 0:
        result = steps_of(key, dims, shards, -0.22, 0.18) * result
    return jnp.clip(result, min=-bound, max=bound).astype(dtype)


def setup_inputs(seed: int = 0) -> dict:
    arg_keys = jax.random.split(jax.random.key(seed), 9)
    return {
        "hidden_rows": centred(arg_keys[0], (HID, N_DP * N_EXPERT * ROWS), 1.0, 6.0, ((1, 512),)),
        "grad_rows": centred(arg_keys[1], (N_DP * N_EXPERT * ROWS, D), 0.03, 0.1796875, ((0, 512),)),
        "block_slot": with_ends(jax.random.randint(arg_keys[2], (N_DP * N_EXPERT, BLOCKS), 0, 2), jax.random.fold_in(arg_keys[2], 1), 0, 1).astype(jnp.int32),
        "live_rows": with_ends(jax.random.randint(arg_keys[3], (N_DP * N_EXPERT,), ROWS // 8, ROWS + 1), jax.random.fold_in(arg_keys[3], 1), ROWS // 8, ROWS).astype(jnp.int32),
        "replica_plan": with_ends(ranked(arg_keys[4], (N_EXPERT,), EXPERTS, 2), jax.random.fold_in(arg_keys[4], 3), 0, EXPERTS - 1).astype(jnp.int32),
        "master": centred(arg_keys[5], (N_EXPERT, HID, D // QUART), HID ** -0.5, 0.21875, ((0, 64), (1, 8)), jnp.float32),
        "moment_one": centred(arg_keys[6], (N_EXPERT, HID, D // QUART), 0.3, 1.8, ((0, 64), (1, 8)), jnp.float32),
        "moment_two": jnp.clip(jnp.exp(math.log(1.0) - 4.6051702 * jax.random.uniform(arg_keys[7], (N_EXPERT, HID, D // QUART), jnp.float32) ** steps_of(arg_keys[7], (N_EXPERT, HID, D // QUART), ((0, 64), (1, 8)), -0.2, 0.2)), 0.01, 1.0),
    }


beta_one = 0.9
beta_two = 0.95
learn_rate = 0.01
decay_rate = 0.1
epsilon = 1e-08
step_count = 10.0

def adam_update(weights, first, second, gradient):
    first_next = beta_one * first + (1.0 - beta_one) * gradient
    second_next = beta_two * second + (1.0 - beta_two) * gradient * gradient
    scaled_first = first_next / (1.0 - beta_one ** step_count)
    scaled_second = second_next / (1.0 - beta_two ** step_count)
    direction = scaled_first / (jnp.sqrt(scaled_second) + epsilon)
    weights_next = weights - learn_rate * (direction + decay_rate * weights)
    return (weights_next, first_next, second_next)

def add_into(total, index, term):
    current = lax.dynamic_index_in_dim(total, index, 0, False)
    return lax.dynamic_update_index_in_dim(total, current + term, index, 0)

def reference(hidden_rows, grad_rows, block_slot, live_rows, replica_plan, master, moment_one, moment_two):
    device_count = N_DP * N_EXPERT
    tok_rows = BLK * BLOCKS
    expert_total = N_EXPERT // QUART
    block_width = D // QUART
    hidden_all = jnp.transpose(hidden_rows.reshape(HID, device_count, tok_rows), (1, 0, 2))
    grad_all = grad_rows.reshape(device_count, tok_rows, D)
    positions = lax.iota(jnp.int32, tok_rows)

    def one_device(total, inputs):
        hidden_dev, grad_dev, slots, live, index = inputs
        kept_rows = positions < live
        row_slot = jnp.repeat(slots, BLK)
        zeros_like = jnp.zeros_like(grad_dev)
        grad_primary = jnp.where((kept_rows & (row_slot == 0))[:, None], grad_dev, zeros_like)
        grad_replica = jnp.where((kept_rows & (row_slot == 1))[:, None], grad_dev, zeros_like)
        primary = jnp.dot(hidden_dev, grad_primary, preferred_element_type=jnp.float32)
        replica_low = lax.optimization_barrier(jnp.dot(hidden_dev, grad_replica, preferred_element_type=jnp.float32).astype(jnp.bfloat16))
        replica = replica_low.astype(jnp.float32)
        column = (index % N_EXPERT).astype(jnp.int32)
        owner = (column % expert_total).astype(jnp.int32)
        host = lax.dynamic_index_in_dim(replica_plan, column, 0, False).astype(jnp.int32)
        total = add_into(total, owner, primary)
        total = add_into(total, host, replica)
        return (total, None)
    start = jnp.zeros((expert_total, HID, D), jnp.float32)
    indices = lax.iota(jnp.int32, device_count)
    gradient, unused = lax.scan(one_device, start, (hidden_all, grad_all, block_slot, live_rows, indices))
    grad_state = jnp.transpose(gradient.reshape(expert_total, HID, QUART, block_width), (2, 0, 1, 3)).reshape(N_EXPERT, HID, block_width)
    master_new, first_new, second_new = adam_update(master, moment_one, moment_two, grad_state)
    full_weights = jnp.transpose(master_new.reshape(QUART, expert_total, HID, block_width), (1, 2, 0, 3)).reshape(expert_total, HID, D)
    replica_weight = jnp.take(full_weights.astype(jnp.bfloat16), replica_plan, axis=0)
    return (master_new, first_new, second_new, replica_weight)
```

```python
import functools

import jax
import jax.numpy as jnp
from jax import lax
from jax.experimental import pallas as pl
from jax.experimental.pallas import tpu as pltpu
from jax.sharding import PartitionSpec as P

MESH = pl.DeviceIdType.MESH

N_Y, N_X, N_C, N_LO, N_HI = 4, 4, 2, 8, 2
N_Z = N_HI * N_LO
N_HOST = N_X * N_C
QUART = 4
EXPERTS = 16
FLAG_ROWS = 16
SUBS = 3

beta_one = 0.9
beta_two = 0.95
learn_rate = 0.01
decay_rate = 0.1
epsilon = 1e-08
step_count = 10.0


def adam_update(weights, first, second, gradient):
    first_next = beta_one * first + (1.0 - beta_one) * gradient
    second_next = beta_two * second + (1.0 - beta_two) * gradient * gradient
    scaled_first = first_next / (1.0 - beta_one**step_count)
    scaled_second = second_next / (1.0 - beta_two**step_count)
    direction = scaled_first / (jnp.sqrt(scaled_second) + epsilon)
    weights_next = weights - learn_rate * (direction + decay_rate * weights)
    return (weights_next, first_next, second_next)


def place():
    g = lax.axis_index("dp")
    j = lax.axis_index("expert")
    z_hi, y = lax.div(g, N_Y), lax.rem(g, N_Y)
    z_lo, x, c = lax.div(j, N_HOST), lax.rem(lax.div(j, N_C), N_X), lax.rem(j, N_C)
    return z_hi, z_lo, y, x, c


def device(z_hi, z_lo, y, x, c):
    return (z_hi * N_Y + y, z_lo * N_HOST + x * N_C + c)


def wrap(v, n):
    return lax.rem(v + n, n)


def slot_at(p, x, c):
    return lax.rem(5 * p + 6 + 4 * x + 8 * c, EXPERTS)


def position_of(e, x, c):
    return lax.rem(13 * (e + 42 - 4 * x - 8 * c), N_Z)


def gradient_kernel(
    plan_ref, hid_ref, grad_ref, out_ref,
    hall, gall, prim, repl, term, ring,
    own_sem, hs1, hr1, hs2, hr2, gs_x, gs_y, gs_h, gs_c, gr, rs, rr, fs, fr,
):
    z_hi, z_lo, y, x, c = place()
    z = z_hi * N_LO + z_lo
    rows, width = out_ref.shape
    half = rows // 2
    sub = half // SUBS
    tok = grad_ref.shape[0]
    up, down = wrap(z + 1, N_Z), wrap(z - 1, N_Z)
    dev_up = device(lax.div(up, N_LO), lax.rem(up, N_LO), y, x, c)
    dev_down = device(lax.div(down, N_LO), lax.rem(down, N_LO), y, x, c)
    e_mine = slot_at(z, x, c)
    dev_to = device(
        c, 2 * x + lax.div(e_mine, N_HOST), y,
        lax.rem(lax.div(e_mine, N_C), N_X), lax.rem(e_mine, N_C),
    )
    e_own = lax.rem(z_lo, 2) * N_HOST + x * N_C + c
    x_from = lax.div(z_lo, 2)
    z_from = position_of(e_own, x_from, z_hi)
    dev_from = device(lax.div(z_from, N_LO), lax.rem(z_from, N_LO), y, x_from, z_hi)

    def here(yy, xx, cc):
        return device(z_hi, z_lo, yy, xx, cc)

    y_next, y_prev = wrap(y + 1, N_Y), wrap(y - 1, N_Y)
    partner = here(y, x, 1 - c)
    yc_peers = [
        (wrap(y + dy, N_Y), c if dc == 0 else 1 - c)
        for dy in range(N_Y) for dc in range(N_C) if (dy, dc) != (0, 0)
    ]
    x_peers = [wrap(x + dx, N_X) for dx in range(1, N_X)]
    me8 = y * N_C + c

    def source(yy, xx, cc):
        return (yy * N_X + xx) * N_C + cc

    own_cols = pl.ds(pl.multiple_of(x * width, 128), width)
    own_g = pltpu.make_async_copy(grad_ref.at[:, own_cols], gall.at[source(y, x, c)], own_sem.at[0])
    own_h = pltpu.make_async_copy(hid_ref.at[c * N_Y + y], hall.at[x, me8], own_sem.at[1])
    own_g.start()
    own_h.start()

    barrier = pltpu.get_barrier_semaphore()
    greeted = [here(yy, x, cc) for yy, cc in yc_peers] + [here(y, xx, c) for xx in x_peers]
    greeted += [dev_up, dev_down, dev_to, dev_from]
    for dev in greeted:
        pl.semaphore_signal(barrier, inc=1, device_id=dev, device_id_type=MESH)
    pl.semaphore_wait(barrier, len(greeted))

    def remote(src, dst, ssem, rsem, dev):
        return pltpu.make_async_remote_copy(
            src_ref=src, dst_ref=dst, send_sem=ssem, recv_sem=rsem,
            device_id=dev, device_id_type=MESH,
        )

    h1 = []
    for k, (yy, cc) in enumerate(yc_peers):
        h1.append(remote(hid_ref.at[cc * N_Y + yy], hall.at[x, me8], hs1.at[k], hr1.at[k], here(yy, x, cc)))
        h1[-1].start()
    gx = []
    for k, xx in enumerate(x_peers):
        cols = pl.ds(pl.multiple_of(xx * width, 128), width)
        s = source(y, x, c)
        gx.append(remote(grad_ref.at[:, cols], gall.at[s], gs_x.at[k], gr.at[k + 1, 0], here(y, xx, c)))
        gx[-1].start()

    prim[...] = jnp.zeros_like(prim)
    repl[...] = jnp.zeros_like(repl)

    own_h.wait()
    for copy in h1:
        copy.wait_recv()
    h2 = []
    for k, xx in enumerate(x_peers):
        h2.append(remote(hall.at[x], hall.at[x], hs2.at[k], hr2.at[k], here(y, xx, c)))
        h2[-1].start()

    def add_product(yy, xx, cc):
        block = hall.at[xx, yy * N_C + cc]
        product = jnp.dot(
            block[pl.ds(0, rows), :], gall[source(yy, xx, cc)], preferred_element_type=jnp.float32
        )
        flag = block[pl.ds(rows, FLAG_ROWS), :].astype(jnp.float32)[0:1, :]
        flag = jnp.concatenate([jnp.broadcast_to(flag, (rows, 128))] * (width // 128), axis=1)
        host = xx * N_C + cc
        rounded = product.astype(jnp.bfloat16).astype(jnp.float32)
        prim[host] += jnp.where(flag > 0.5, 0.0, product)
        repl[host] += jnp.where(flag > 0.5, rounded, 0.0)

    top, bottom = pl.ds(0, tok // 2), pl.ds(tok // 2, tok // 2)

    def to_partner(group, dx, s):
        return remote(gall.at[s], gall.at[s], gs_c.at[group, dx], gr.at[(4 + group) * 4 + dx, 0], partner)

    def full(s, group, dx, dev):
        return remote(gall.at[s], gall.at[s], gs_y.at[0, dx], gr.at[group * 4 + dx, 0], dev)

    def group_own(dx, carry):
        xx = wrap(x - dx, N_X)
        s = source(y, xx, c)

        @pl.when(dx == 0)
        def _():
            own_g.wait()

        @pl.when(dx > 0)
        def _():
            full(s, 0, dx, partner).wait_recv()

        remote(gall.at[s], gall.at[s], gs_y.at[0, dx], gr.at[4 + dx, 0], here(y_next, x, c)).start()
        remote(gall.at[s], gall.at[s], gs_y.at[1, dx], gr.at[8 + dx, 0], here(y_prev, x, c)).start()
        to_partner(0, dx, s).start()

        @pl.when(dx == 0)
        def _():
            for copy in h2:
                copy.wait_recv()

        add_product(y, xx, c)
        return carry

    lax.fori_loop(0, N_X, group_own, 0)

    def group_prev(dx, carry):
        xx = wrap(x - dx, N_X)
        s = source(y_prev, xx, c)
        full(s, 1, dx, partner).wait_recv()
        remote(
            gall.at[s, top], gall.at[s, top], gs_h.at[0, dx], gr.at[12 + dx, 0], here(y_next, x, c)
        ).start()
        to_partner(1, dx, s).start()
        s2 = source(y_next, xx, c)
        full(s2, 2, dx, partner).wait_recv()
        remote(
            gall.at[s2, bottom], gall.at[s2, bottom], gs_h.at[1, dx], gr.at[12 + dx, 1], here(y_prev, x, c)
        ).start()
        to_partner(2, dx, s2).start()
        add_product(y_prev, xx, c)
        add_product(y_next, xx, c)
        return carry

    lax.fori_loop(0, N_X, group_prev, 0)

    y_far = wrap(y + 2, N_Y)

    def group_far(dx, carry):
        xx = wrap(x - dx, N_X)
        s = source(y_far, xx, c)
        remote(
            gall.at[s, top], gall.at[s, top], gs_h.at[0, dx], gr.at[12 + dx, 0], partner
        ).wait_recv()
        remote(
            gall.at[s, bottom], gall.at[s, bottom], gs_h.at[1, dx], gr.at[12 + dx, 1], partner
        ).wait_recv()
        to_partner(3, dx, s).start()
        add_product(y_far, xx, c)
        return carry

    lax.fori_loop(0, N_X, group_far, 0)

    def group_partner(k, carry):
        group, dx = lax.div(k, N_X), lax.rem(k, N_X)
        yy = wrap(y + jnp.where(group == 1, N_Y - 1, jnp.where(group == 2, 1, jnp.where(group == 3, 2, 0))), N_Y)
        xx = wrap(x - dx, N_X)
        s = source(yy, xx, 1 - c)
        remote(
            gall.at[s], gall.at[s], gs_c.at[group, dx], gr.at[(4 + group) * 4 + dx, 0], partner
        ).wait_recv()
        add_product(yy, xx, 1 - c)
        return carry

    lax.fori_loop(0, 4 * N_X, group_partner, 0)

    parity = lax.rem(z_lo, 2)

    def make_term(s):
        for d in range(2):
            p = wrap(z - 1 - s, N_Z) if d == 0 else wrap(z + 1 + s, N_Z)
            p = lax.rem(p + N_Z, N_Z)
            e = slot_at(p, x, c)
            span = pl.ds(d * half, half)
            weight = jnp.where(lax.div(e, N_HOST) == parity, 1.0, 0.0)
            total = prim[lax.rem(e, N_HOST), span, :] * weight
            for h in range(N_HOST):
                weight = jnp.where(plan_ref[z_lo * N_HOST + h] == e, 1.0, 0.0)
                total += repl[h, span, :] * weight
            term[d, s] = total

    def ring_copy(d, s, u, src):
        return remote(
            src, ring.at[d, s, pl.ds(u * sub, sub)], rs.at[d, s, u], rr.at[d, s, u],
            dev_up if d == 0 else dev_down,
        )

    make_term(0)
    for u in range(SUBS):
        for d in range(2):
            ring_copy(d, 0, u, term.at[d, 0, pl.ds(u * sub, sub)]).start()
    make_term(1)

    def ring_step(s, carry):
        for u in range(SUBS):
            for d in range(2):
                part = pl.ds(u * sub, sub)
                ring_copy(d, s - 1, u, ring.at[d, s - 1, part]).wait_recv()
                ring[d, s - 1, part, :] += term[d, s, part, :]
                ring_copy(d, s, u, ring.at[d, s - 1, part]).start()
        make_term(s + 1)
        return carry

    lax.fori_loop(1, N_Z - 1, ring_step, 0)

    last = []
    for u in range(SUBS):
        for d in range(2):
            part = pl.ds(u * sub, sub)
            ring_copy(d, N_Z - 2, u, ring.at[d, N_Z - 2, part]).wait_recv()
            ring[d, N_Z - 2, part, :] += term[d, N_Z - 1, part, :]
            copy = remote(
                ring.at[d, N_Z - 2, part], out_ref.at[pl.ds(d * half + u * sub, sub)],
                fs.at[d, u], fr.at[d, u], dev_to,
            )
            copy.start()
            last.append(copy)

    for copy in h1 + h2 + gx:
        copy.wait_send()

    def drain(dx, carry):
        whole = gall.at[source(y, x, c)]
        part = gall.at[source(y, x, c), top]
        for k in range(2):
            remote(whole, whole, gs_y.at[k, dx], gr.at[0, 0], partner).wait_send()
            remote(part, part, gs_h.at[k, dx], gr.at[0, 0], partner).wait_send()
        for k in range(4):
            remote(whole, whole, gs_c.at[k, dx], gr.at[0, 0], partner).wait_send()
        return carry

    lax.fori_loop(0, N_X, drain, 0)

    def drain_ring(s, carry):
        for u in range(SUBS):
            for d in range(2):
                ring_copy(d, s, u, term.at[d, 0, pl.ds(u * sub, sub)]).wait_send()
        return carry

    lax.fori_loop(0, N_Z - 1, drain_ring, 0)
    for copy in last:
        copy.wait()


def weights_kernel(plan_ref, fresh_ref, out_ref, line, mixed, picked, own_sem, ls, lr, ms, mr, ps, pr):
    z_hi, z_lo, y, x, c = place()
    rows, width = fresh_ref.shape
    half = rows // 2

    def here(zz, xx, cc):
        return device(z_hi, zz, y, xx, cc)

    right, left = wrap(z_lo + 1, N_LO), wrap(z_lo - 1, N_LO)
    plane = [(dx, dc) for dx in range(N_X) for dc in range(N_C)]

    def peer(dx, dc):
        return wrap(x + dx, N_X), (c if dc == 0 else 1 - c)

    own = pltpu.make_async_copy(fresh_ref, line.at[z_lo], own_sem.at[0])
    own.start()
    barrier = pltpu.get_barrier_semaphore()
    greeted = [here(z_lo, *peer(dx, dc)) for dx, dc in plane[1:]]
    greeted += [here(right, x, c), here(left, x, c)]
    for dev in greeted:
        pl.semaphore_signal(barrier, inc=1, device_id=dev, device_id_type=MESH)
    pl.semaphore_wait(barrier, len(greeted))
    own.wait()

    def remote(src, dst, ssem, rsem, dev):
        return pltpu.make_async_remote_copy(
            src_ref=src, dst_ref=dst, send_sem=ssem, recv_sem=rsem,
            device_id=dev, device_id_type=MESH,
        )

    def line_copy(d, k):
        return remote(line.at[k], line.at[k], ls.at[d, k], lr.at[k], here(right if d == 0 else left, x, c))

    def mix_copy(k, cc):
        q, b = lax.div(k, 2), lax.rem(k, 2)
        e = b * N_HOST + x * N_C + c
        dist = wrap(q - x, N_X)
        apart = jnp.where(cc == c, 0, 1)
        src = line.at[k, pl.ds(cc * half, half)]
        return remote(
            src, mixed.at[e], ms.at[k, cc], mr.at[b, dist, apart], here(z_lo, q, cc)
        )

    def local_mix(k):
        b = lax.rem(k, 2)
        return pltpu.make_async_copy(
            line.at[k, pl.ds(pl.multiple_of(c * half, 16), half)],
            mixed.at[b * N_HOST + x * N_C + c], own_sem.at[1 + b],
        )

    def scatter(k):
        q = lax.div(k, 2)
        for cc in range(N_C):
            mine = (q == x) & (cc == c)

            @pl.when(mine)
            def _():
                local_mix(k).start()

            @pl.when(jnp.logical_not(mine))
            def _():
                mix_copy(k, cc).start()

    @pl.when(z_lo < N_LO - 1)
    def _():
        line_copy(0, z_lo).start()

    @pl.when(z_lo > 0)
    def _():
        line_copy(1, z_lo).start()

    scatter(z_lo)

    def line_step(t, carry):
        k = z_lo - t

        @pl.when(k >= 0)
        def _():
            line_copy(0, k).wait_recv()

            @pl.when(z_lo < N_LO - 1)
            def _():
                line_copy(0, k).start()

            scatter(k)

        k2 = z_lo + t

        @pl.when(k2 < N_LO)
        def _():
            line_copy(1, k2).wait_recv()

            @pl.when(z_lo > 0)
            def _():
                line_copy(1, k2).start()

            scatter(k2)

        return carry

    lax.fori_loop(1, N_LO, line_step, 0)

    for b in range(2):
        local_mix(2 * x + b).wait()
        for dx, dc in plane[1:]:
            piece = mixed.at[0]
            remote(piece, piece, ms.at[0, 0], mr.at[b, dx, dc], here(z_lo, *peer(1, 0))).wait_recv()

    mine = out_ref.at[pl.ds(pl.multiple_of(c * half, 16), half), pl.ds(pl.multiple_of(x * width, 128), width)]
    sends = []
    for n, (dx, dc) in enumerate(plane):
        xx, cc = peer(dx, dc)
        picked[n] = mixed[plan_ref[z_lo * N_HOST + xx * N_C + cc]]
        if n == 0:
            sends.append(pltpu.make_async_copy(picked.at[0], mine, own_sem.at[3]))
        else:
            sends.append(remote(picked.at[n], mine, ps.at[n], pr.at[n], here(z_lo, xx, cc)))
        sends[-1].start()

    def drain(k, carry):
        @pl.when((z_lo < N_LO - 1) & (k <= z_lo))
        def _():
            line_copy(0, k).wait_send()

        @pl.when((z_lo > 0) & (k >= z_lo))
        def _():
            line_copy(1, k).wait_send()

        for cc in range(N_C):
            @pl.when(jnp.logical_not((lax.div(k, 2) == x) & (cc == c)))
            def _():
                mix_copy(k, cc).wait_send()

        return carry

    lax.fori_loop(0, N_LO, drain, 0)
    for copy in sends:
        copy.wait()


def per_device(
    hidden_rows, grad_rows, block_slot, live_rows, replica_plan, master, moment_one, moment_two
):
    hidden_units, tok = hidden_rows.shape
    model_width = grad_rows.shape[1]
    groups = N_HI * N_Y
    rows = hidden_units // groups
    width = model_width // QUART
    half = rows // 2
    kept = lax.iota(jnp.int32, tok) < live_rows[0]
    masked = jnp.where(kept[None, :], hidden_rows, jnp.zeros_like(hidden_rows)).reshape(groups, rows, tok)
    flags = jnp.broadcast_to((block_slot[0, 0] == 1).astype(jnp.bfloat16), (groups, FLAG_ROWS, tok))
    hid = jnp.concatenate([masked, flags], axis=1)
    sub = half // SUBS
    dma = pltpu.SemaphoreType.DMA
    gradient = pl.pallas_call(
        gradient_kernel,
        out_shape=jax.ShapeDtypeStruct((rows, width), jnp.float32),
        in_specs=[
            pl.BlockSpec(memory_space=pltpu.SMEM),
            pl.BlockSpec(memory_space=pl.ANY),
            pl.BlockSpec(memory_space=pl.ANY),
        ],
        out_specs=pl.BlockSpec(memory_space=pltpu.VMEM),
        scratch_shapes=[
            pltpu.VMEM((N_X, N_Y * N_C, rows + FLAG_ROWS, tok), jnp.bfloat16),
            pltpu.VMEM((N_Y * N_X * N_C, tok, width), jnp.bfloat16),
            pltpu.VMEM((N_HOST, rows, width), jnp.float32),
            pltpu.VMEM((N_HOST, rows, width), jnp.float32),
            pltpu.VMEM((2, N_Z, half, width), jnp.float32),
            pltpu.VMEM((2, N_Z - 1, half, width), jnp.float32),
            dma((2,)), dma((7,)), dma((7,)), dma((3,)), dma((3,)),
            dma((3,)), dma((2, 4)), dma((2, 4)), dma((4, 4)), dma((32, 2)),
            dma((2, N_Z - 1, SUBS)), dma((2, N_Z - 1, SUBS)), dma((2, SUBS)), dma((2, SUBS)),
        ],
        compiler_params=pltpu.CompilerParams(
            collective_id=0, has_side_effects=True, vmem_limit_bytes=40 * 2**20
        ),
        name="gradient",
    )(replica_plan, hid, grad_rows)
    weights_next, first_next, second_next = adam_update(
        master[0], moment_one[0], moment_two[0], gradient
    )
    fresh = weights_next.astype(jnp.bfloat16)
    replica_weight = pl.pallas_call(
        weights_kernel,
        out_shape=jax.ShapeDtypeStruct((rows, model_width), jnp.bfloat16),
        in_specs=[
            pl.BlockSpec(memory_space=pltpu.SMEM),
            pl.BlockSpec(memory_space=pltpu.VMEM),
        ],
        out_specs=pl.BlockSpec(memory_space=pltpu.VMEM),
        scratch_shapes=[
            pltpu.VMEM((N_LO, rows, width), jnp.bfloat16),
            pltpu.VMEM((EXPERTS, half, width), jnp.bfloat16),
            pltpu.VMEM((N_HOST, half, width), jnp.bfloat16),
            dma((4,)), dma((2, N_LO)), dma((N_LO,)), dma((N_LO, N_C)), dma((2, N_X, N_C)),
            dma((N_HOST,)), dma((N_HOST,)),
        ],
        compiler_params=pltpu.CompilerParams(
            collective_id=1, has_side_effects=True, vmem_limit_bytes=16 * 2**20
        ),
        name="weights",
    )(replica_plan, fresh)
    return (weights_next[None], first_next[None], second_next[None], replica_weight[None])


def solution(mesh):
    return jax.shard_map(
        per_device,
        mesh=mesh,
        in_specs=(
            P(None, ("dp", "expert")),
            P(("dp", "expert"), None),
            P(("dp", "expert"), None),
            P(("dp", "expert")),
            P(),
            P("expert", "dp", None),
            P("expert", "dp", None),
            P("expert", "dp", None),
        ),
        out_specs=(
            P("expert", "dp", None),
            P("expert", "dp", None),
            P("expert", "dp", None),
            P("expert", "dp", None),
        ),
        check_vma=False,
    )
```

```python
import functools

import jax
import jax.numpy as jnp
from jax import lax
from jax.experimental import pallas as pl
from jax.experimental.pallas import tpu as pltpu
from jax.sharding import PartitionSpec as P

MESH = pl.DeviceIdType.MESH

N_Y, N_X, N_C, N_LO, N_HI = 4, 4, 2, 8, 2
N_Z = N_HI * N_LO
N_HOST = N_X * N_C
QUART = 4
EXPERTS = 16
FLAG_ROWS = 16
CHUNKS = ((0, 384), (384, 256))

beta_one = 0.9
beta_two = 0.95
learn_rate = 0.01
decay_rate = 0.1
epsilon = 1e-08
step_count = 10.0


def adam_update(weights, first, second, gradient):
    first_next = beta_one * first + (1.0 - beta_one) * gradient
    second_next = beta_two * second + (1.0 - beta_two) * gradient * gradient
    scaled_first = first_next / (1.0 - beta_one**step_count)
    scaled_second = second_next / (1.0 - beta_two**step_count)
    direction = scaled_first / (jnp.sqrt(scaled_second) + epsilon)
    weights_next = weights - learn_rate * (direction + decay_rate * weights)
    return (weights_next, first_next, second_next)


def place():
    g = lax.axis_index("dp")
    j = lax.axis_index("expert")
    z_hi, y = lax.div(g, N_Y), lax.rem(g, N_Y)
    z_lo, x, c = lax.div(j, N_HOST), lax.rem(lax.div(j, N_C), N_X), lax.rem(j, N_C)
    return z_hi, z_lo, y, x, c


def device(z_hi, z_lo, y, x, c):
    return (z_hi * N_Y + y, z_lo * N_HOST + x * N_C + c)


def wrap(v, n):
    return lax.rem(v + n, n)


def gradient_kernel(
    plan_ref, hid_ref, grad_ref, out_ref,
    hall, gall, prim, repl, ring,
    own_sem, hs1, hr1, hs2, hr2, gxs, gr, gys, gyh, gcs, gcr, rs, rr, fs, fr,
):
    z_hi, z_lo, y, x, c = place()
    z = z_hi * N_LO + z_lo
    rows, width = out_ref.shape
    half = rows // 2
    tok = grad_ref.shape[0]

    def here(yy, xx, cc):
        return device(z_hi, z_lo, yy, xx, cc)

    def level(zz):
        return device(lax.div(zz, N_LO), lax.rem(zz, N_LO), y, x, c)

    y_next, y_prev, y_far = wrap(y + 1, N_Y), wrap(y - 1, N_Y), wrap(y + 2, N_Y)
    partner = here(y, x, 1 - c)
    yc_peers = [
        (wrap(y + dy, N_Y), c if dc == 0 else 1 - c)
        for dy in range(N_Y) for dc in range(N_C) if (dy, dc) != (0, 0)
    ]
    x_peers = [wrap(x + dx, N_X) for dx in range(1, N_X)]
    xc_peers = [(xx, cc) for xx in x_peers for cc in (c, 1 - c)]
    me8 = y * N_C + c

    def source(yy, xx, cc):
        return (yy * N_X + xx) * N_C + cc

    me = source(y, x, c)

    def columns(q, ch):
        return pl.ds(pl.multiple_of(q * width + CHUNKS[ch][0], 128), CHUNKS[ch][1])

    def span(ch):
        return pl.ds(*CHUNKS[ch])

    own_cols = pl.ds(pl.multiple_of(x * width, 128), width)
    own_g = pltpu.make_async_copy(grad_ref.at[:, own_cols], gall.at[me], own_sem.at[0])
    own_h = pltpu.make_async_copy(hid_ref.at[c * N_Y + y], hall.at[x, me8], own_sem.at[1])
    own_h.start()
    own_g.start()

    barrier = pltpu.get_barrier_semaphore()
    greeted = [here(yy, x, cc) for yy, cc in yc_peers] + [here(y, xx, cc) for xx, cc in xc_peers]
    greeted += [level(wrap(z + 1, N_Z)), level(wrap(z - 1, N_Z))]
    for dev in greeted:
        pl.semaphore_signal(barrier, inc=1, device_id=dev, device_id_type=MESH)
    pl.semaphore_wait(barrier, len(greeted))

    def remote(src, dst, ssem, rsem, dev):
        return pltpu.make_async_remote_copy(
            src_ref=src, dst_ref=dst, send_sem=ssem, recv_sem=rsem,
            device_id=dev, device_id_type=MESH,
        )

    def loop(first, count, body):
        def one(k, carry):
            body(k)
            return carry

        lax.fori_loop(first, first + count, one, 0)

    parts = (pl.ds(0, tok // 2), pl.ds(tok // 2, tok // 2))
    rows_of = (y, y_prev, y_next, y_far)

    def origin(group, dx):
        return rows_of[group], wrap(x - dx, N_X)

    def along_x(dx, ch):
        xx = wrap(x + dx, N_X)
        return remote(
            grad_ref.at[:, columns(xx, ch)], gall.at[me, :, span(ch)],
            gxs.at[ch, dx - 1], gr.at[ch, dx, 0], here(y, xx, c),
        )

    def along_y(way, dx, ch):
        yy, xx = origin(0, dx)
        piece = gall.at[source(yy, xx, c), :, span(ch)]
        return remote(
            piece, piece, gys.at[ch, way, dx], gr.at[ch, (1 + way) * N_X + dx, 0],
            here(y_next if way == 0 else y_prev, x, c),
        )

    def onward(way, dx, ch):
        yy, xx = origin(1 + way, dx)
        piece = gall.at[source(yy, xx, c), parts[way], span(ch)]
        return remote(
            piece, piece, gyh.at[ch, way, dx], gr.at[ch, 3 * N_X + dx, way],
            here(y_next if way == 0 else y_prev, x, c),
        )

    def across(group, dx, ch):
        yy, xx = origin(group, dx)
        piece = gall.at[source(yy, xx, c), :, span(ch)]
        return remote(piece, piece, gcs.at[ch, group, dx], gcr.at[ch, group, dx], partner)

    def arrive(group, dx, ch):
        yy, xx = origin(group, dx)
        if group < 3:
            piece = gall.at[source(yy, xx, c), :, span(ch)]
            remote(piece, piece, gys.at[ch, 0, dx], gr.at[ch, group * N_X + dx, 0], partner).wait_recv()
        else:
            for part in range(2):
                piece = gall.at[source(yy, xx, c), parts[part], span(ch)]
                remote(piece, piece, gys.at[ch, 0, dx], gr.at[ch, 3 * N_X + dx, part], partner).wait_recv()

    def spread_own(dx, ch):
        along_y(0, dx, ch).start()
        along_y(1, dx, ch).start()
        across(0, dx, ch).start()

    def take_x(dx, ch):
        arrive(0, dx, ch)
        spread_own(dx, ch)

    def take_y(dx, ch):
        for way in range(2):
            arrive(1 + way, dx, ch)
            onward(way, dx, ch).start()
            across(1 + way, dx, ch).start()

    def take_far(dx, ch):
        arrive(3, dx, ch)
        across(3, dx, ch).start()

    def add_product(yy, xx, cc, ch):
        block = hall.at[xx, yy * N_C + cc]
        product = jnp.dot(
            block[pl.ds(0, rows), :], gall[source(yy, xx, cc), :, span(ch)], preferred_element_type=jnp.float32
        )
        flag = block[pl.ds(rows, FLAG_ROWS), :].astype(jnp.float32)[0:1, :]
        flag = jnp.concatenate([jnp.broadcast_to(flag, (rows, 128))] * (CHUNKS[ch][1] // 128), axis=1)
        host = xx * N_C + cc
        rounded = product.astype(jnp.bfloat16).astype(jnp.float32)
        prim[host, :, span(ch)] += jnp.where(flag > 0.5, 0.0, product)
        repl[host, :, span(ch)] += jnp.where(flag > 0.5, rounded, 0.0)

    def rail_product(group, dx, ch):
        add_product(*origin(group, dx), c, ch)

    def take_across(k, ch):
        group, dx = lax.div(k, N_X), lax.rem(k, N_X)
        dy = jnp.where(group == 1, N_Y - 1, jnp.where(group == 2, 1, jnp.where(group == 3, 2, 0)))
        yy, xx = wrap(y + dy, N_Y), wrap(x - dx, N_X)
        piece = gall.at[source(yy, xx, 1 - c), :, span(ch)]
        remote(piece, piece, gcs.at[ch, group, dx], gcr.at[ch, group, dx], partner).wait_recv()
        add_product(yy, xx, 1 - c, ch)

    h1 = []
    for k, (yy, cc) in enumerate(yc_peers):
        h1.append(remote(hid_ref.at[cc * N_Y + yy], hall.at[x, me8], hs1.at[k], hr1.at[k], here(yy, x, cc)))
        h1[-1].start()
    for dx in range(1, N_X):
        along_x(dx, 0).start()
    own_g.wait()
    spread_own(0, 0)
    prim[...] = jnp.zeros_like(prim)
    repl[...] = jnp.zeros_like(repl)
    own_h.wait()
    for copy in h1:
        copy.wait_recv()
    h2 = []
    for k, xx in enumerate(x_peers):
        h2.append(remote(hall.at[x], hall.at[x], hs2.at[k], hr2.at[k], here(y, xx, c)))
        h2[-1].start()
    for dx in range(1, N_X):
        along_x(dx, 1).start()
    loop(1, N_X - 1, lambda dx: take_x(dx, 0))
    loop(0, N_X, lambda dx: take_y(dx, 0))
    for copy in h2:
        copy.wait_recv()
    for group in range(3):
        loop(0, N_X, lambda dx, group=group: rail_product(group, dx, 0))

    def far_first(dx):
        take_far(dx, 0)
        rail_product(3, dx, 0)

    loop(0, N_X, far_first)
    loop(0, 4 * N_X, lambda k: take_across(k, 0))

    parity = lax.rem(z_lo, 2)

    def addend(e, part, ch):
        weight = jnp.where(lax.div(e, N_HOST) == parity, 1.0, 0.0)
        total = prim[lax.rem(e, N_HOST), part, span(ch)] * weight
        for h in range(N_HOST):
            weight = jnp.where(plan_ref[z_lo * N_HOST + h] == e, 1.0, 0.0)
            total += repl[h, part, span(ch)] * weight
        return total

    offset = [wrap(z - (8 * c + 2 * x + b), N_Z) for b in range(2)]
    lag = [jnp.where(r >= 8, r - 8, jnp.where(r == 0, 8, 7 - r)) for r in offset]

    def hop(e, ch, hf, r):
        way = jnp.where(r >= 8, 0, 1)
        piece = ring.at[way, e, pl.ds(hf * half, half), span(ch)]
        return remote(
            piece, piece, rs.at[ch, hf, e], rr.at[way, ch, hf, e], level(wrap(jnp.where(r >= 8, z + 1, z - 1), N_Z))
        )

    def landed(e, ch, hf, way):
        piece = ring.at[way, e, pl.ds(hf * half, half), span(ch)]
        remote(piece, piece, rs.at[ch, hf, e], rr.at[way, ch, hf, e], partner).wait_recv()

    def deliver(e, ch, hf):
        part = pl.ds(hf * half, half)
        xx, cc = lax.rem(lax.div(e, N_C), N_X), lax.rem(e, N_C)
        return remote(
            ring.at[0, e, part, span(ch)], out_ref.at[part, span(ch)], fs.at[ch, hf, e], fr.at[ch, hf], here(y, xx, cc)
        )

    def keep(e, ch, hf):
        part = pl.ds(hf * half, half)
        return pltpu.make_async_copy(ring.at[0, e, part, span(ch)], out_ref.at[part, span(ch)], fr.at[ch, hf])

    def mine(e):
        return lax.rem(e, N_HOST) == x * N_C + c

    def unit(e, ch, r):
        for hf in range(2):
            part = pl.ds(hf * half, half)
            way = jnp.where(r >= 8, 0, 1)

            @pl.when((r == 7) | (r == 8))
            def _():
                ring[way, e, part, span(ch)] = addend(e, part, ch)

            @pl.when((r != 7) & (r != 8) & (r != 0))
            def _():
                landed(e, ch, hf, way)
                ring[way, e, part, span(ch)] += addend(e, part, ch)

            @pl.when(r != 0)
            def _():
                hop(e, ch, hf, r).start()

            @pl.when(r == 0)
            def _():
                landed(e, ch, hf, 0)
                landed(e, ch, hf, 1)
                ring[0, e, part, span(ch)] += ring[1, e, part, span(ch)] + addend(e, part, ch)

                @pl.when(mine(e))
                def _():
                    keep(e, ch, hf).start()

                @pl.when(jnp.logical_not(mine(e)))
                def _():
                    deliver(e, ch, hf).start()

    def units(i):
        for ch in range(2):
            for b in range(2):
                first = EXPERTS * ch + N_HOST * b
                n = i - lag[b]

                @pl.when((n >= first) & (n < first + N_HOST))
                def _():
                    unit(n - EXPERTS * ch, ch, offset[b])


    def step_x(i):
        @pl.when(i > 0)
        def _():
            arrive(0, i, 1)

        spread_own(i, 1)
        rail_product(0, i, 1)
        units(i)

    def step_y(i):
        take_y(i - 4, 1)
        rail_product(1, i - 4, 1)
        rail_product(2, i - 4, 1)
        units(i)

    def step_far(i):
        take_far(i - 8, 1)
        rail_product(3, i - 8, 1)
        units(i)

    def step_across(i):
        loop(4 * (i - 12), 4, lambda k: take_across(k, 1))
        units(i)

    for first, step in ((0, step_x), (4, step_y), (8, step_far), (12, step_across)):
        loop(first, 4, step)
    loop(16, 2 * EXPERTS + 8 - 15, units)

    for copy in h1 + h2:
        copy.wait_send()
    for ch in range(2):
        def drain(dx, ch=ch):
            for way in range(2):
                along_y(way, dx, ch).wait_send()
                onward(way, dx, ch).wait_send()
            for group in range(4):
                across(group, dx, ch).wait_send()

        for dx in range(1, N_X):
            along_x(dx, ch).wait_send()
        loop(0, N_X, drain)

        def drain_units(e, ch=ch):
            b = lax.div(e, N_HOST)
            r = jnp.where(b == 0, offset[0], offset[1])
            for hf in range(2):
                @pl.when(r != 0)
                def _():
                    hop(e, ch, hf, r).wait_send()

                @pl.when((r == 0) & jnp.logical_not(mine(e)))
                def _():
                    deliver(e, ch, hf).wait_send()

        loop(0, EXPERTS, drain_units)
    kept = (x == lax.div(z_lo, 2)) & (c == z_hi)
    e_own = parity * N_HOST + x * N_C + c
    for ch in range(2):
        for hf in range(2):
            @pl.when(kept)
            def _():
                keep(e_own, ch, hf).wait()

            @pl.when(jnp.logical_not(kept))
            def _():
                deliver(e_own, ch, hf).wait_recv()


def weights_kernel(plan_ref, fresh_ref, out_ref, line, mixed, picked, own_sem, ls, lr, ms, mr, ps, pr):
    z_hi, z_lo, y, x, c = place()
    rows, width = fresh_ref.shape
    half = rows // 2

    def here(zz, xx, cc):
        return device(z_hi, zz, y, xx, cc)

    right, left = wrap(z_lo + 1, N_LO), wrap(z_lo - 1, N_LO)
    plane = [(dx, dc) for dx in range(N_X) for dc in range(N_C)]

    def peer(dx, dc):
        return wrap(x + dx, N_X), (c if dc == 0 else 1 - c)

    own = [
        pltpu.make_async_copy(fresh_ref.at[pl.ds(hf * half, half)], line.at[z_lo, hf], own_sem.at[3 + hf])
        for hf in range(2)
    ]
    for copy in own:
        copy.start()
    barrier = pltpu.get_barrier_semaphore()
    greeted = [here(z_lo, *peer(dx, dc)) for dx, dc in plane[1:]]
    greeted += [here(right, x, c), here(left, x, c)]
    for dev in greeted:
        pl.semaphore_signal(barrier, inc=1, device_id=dev, device_id_type=MESH)
    pl.semaphore_wait(barrier, len(greeted))
    for copy in own:
        copy.wait()

    def remote(src, dst, ssem, rsem, dev):
        return pltpu.make_async_remote_copy(
            src_ref=src, dst_ref=dst, send_sem=ssem, recv_sem=rsem,
            device_id=dev, device_id_type=MESH,
        )

    def line_copy(d, k, hf):
        piece = line.at[k, hf]
        return remote(piece, piece, ls.at[d, k, hf], lr.at[k, hf], here(right if d == 0 else left, x, c))

    def mix_copy(k, cc):
        q, b = lax.div(k, 2), lax.rem(k, 2)
        e = b * N_HOST + x * N_C + c
        dist = wrap(q - x, N_X)
        apart = jnp.where(cc == c, 0, 1)
        return remote(line.at[k, cc], mixed.at[e], ms.at[k, cc], mr.at[b, dist, apart], here(z_lo, q, cc))

    def local_mix(k):
        b = lax.rem(k, 2)
        return pltpu.make_async_copy(line.at[k, c], mixed.at[b * N_HOST + x * N_C + c], own_sem.at[1 + b])

    def scatter(k, cc):
        mine = (lax.div(k, 2) == x) & (cc == c)

        @pl.when(mine)
        def _():
            local_mix(k).start()

        @pl.when(jnp.logical_not(mine))
        def _():
            mix_copy(k, cc).start()

    for hf in range(2):
        @pl.when(z_lo < N_LO - 1)
        def _():
            line_copy(0, z_lo, hf).start()

        @pl.when(z_lo > 0)
        def _():
            line_copy(1, z_lo, hf).start()

    for hf in range(2):
        scatter(z_lo, hf)

    def line_step(t, carry):
        k, k2 = z_lo - t, z_lo + t
        for hf in range(2):
            @pl.when(k >= 0)
            def _():
                line_copy(0, k, hf).wait_recv()

                @pl.when(z_lo < N_LO - 1)
                def _():
                    line_copy(0, k, hf).start()

                scatter(k, hf)

            @pl.when(k2 < N_LO)
            def _():
                line_copy(1, k2, hf).wait_recv()

                @pl.when(z_lo > 0)
                def _():
                    line_copy(1, k2, hf).start()

                scatter(k2, hf)

        return carry

    lax.fori_loop(1, N_LO, line_step, 0)

    for b in range(2):
        local_mix(2 * x + b).wait()
        for dx, dc in plane[1:]:
            piece = mixed.at[0]
            remote(piece, piece, ms.at[0, 0], mr.at[b, dx, dc], here(z_lo, *peer(1, 0))).wait_recv()

    mine = out_ref.at[pl.ds(pl.multiple_of(c * half, 16), half), pl.ds(pl.multiple_of(x * width, 128), width)]
    sends = []
    for n, (dx, dc) in enumerate(plane):
        xx, cc = peer(dx, dc)
        picked[n] = mixed[plan_ref[z_lo * N_HOST + xx * N_C + cc]]
        if n == 0:
            sends.append(pltpu.make_async_copy(picked.at[0], mine, own_sem.at[0]))
        else:
            sends.append(remote(picked.at[n], mine, ps.at[n], pr.at[n], here(z_lo, xx, cc)))
        sends[-1].start()

    def drain(k, carry):
        for hf in range(2):
            @pl.when((z_lo < N_LO - 1) & (k <= z_lo))
            def _():
                line_copy(0, k, hf).wait_send()

            @pl.when((z_lo > 0) & (k >= z_lo))
            def _():
                line_copy(1, k, hf).wait_send()

            @pl.when(jnp.logical_not((lax.div(k, 2) == x) & (hf == c)))
            def _():
                mix_copy(k, hf).wait_send()

        return carry

    lax.fori_loop(0, N_LO, drain, 0)
    for copy in sends:
        copy.wait()


def per_device(
    hidden_rows, grad_rows, block_slot, live_rows, replica_plan, master, moment_one, moment_two
):
    hidden_units, tok = hidden_rows.shape
    model_width = grad_rows.shape[1]
    groups = N_HI * N_Y
    rows = hidden_units // groups
    width = model_width // QUART
    half = rows // 2
    kept = lax.iota(jnp.int32, tok) < live_rows[0]
    masked = jnp.where(kept[None, :], hidden_rows, jnp.zeros_like(hidden_rows)).reshape(groups, rows, tok)
    flags = jnp.broadcast_to((block_slot[0, 0] == 1).astype(jnp.bfloat16), (groups, FLAG_ROWS, tok))
    hid = jnp.concatenate([masked, flags], axis=1)
    dma = pltpu.SemaphoreType.DMA
    gradient = pl.pallas_call(
        gradient_kernel,
        out_shape=jax.ShapeDtypeStruct((rows, width), jnp.float32),
        in_specs=[
            pl.BlockSpec(memory_space=pltpu.SMEM),
            pl.BlockSpec(memory_space=pl.ANY),
            pl.BlockSpec(memory_space=pl.ANY),
        ],
        out_specs=pl.BlockSpec(memory_space=pltpu.VMEM),
        scratch_shapes=[
            pltpu.VMEM((N_X, N_Y * N_C, rows + FLAG_ROWS, tok), jnp.bfloat16),
            pltpu.VMEM((N_Y * N_X * N_C, tok, width), jnp.bfloat16),
            pltpu.VMEM((N_HOST, rows, width), jnp.float32),
            pltpu.VMEM((N_HOST, rows, width), jnp.float32),
            pltpu.VMEM((2, EXPERTS, rows, width), jnp.float32),
            dma((2,)), dma((7,)), dma((7,)), dma((3,)), dma((3,)),
            dma((2, 3)), dma((2, 4 * N_X, 2)), dma((2, 2, N_X)), dma((2, 2, N_X)), dma((2, 4, N_X)), dma((2, 4, N_X)),
            dma((2, 2, EXPERTS)), dma((2, 2, 2, EXPERTS)), dma((2, 2, EXPERTS)), dma((2, 2)),
        ],
        compiler_params=pltpu.CompilerParams(
            collective_id=0, has_side_effects=True, vmem_limit_bytes=40 * 2**20
        ),
        name="gradient",
    )(replica_plan, hid, grad_rows)
    weights_next, first_next, second_next = adam_update(
        master[0], moment_one[0], moment_two[0], gradient
    )
    fresh = weights_next.astype(jnp.bfloat16)
    replica_weight = pl.pallas_call(
        weights_kernel,
        out_shape=jax.ShapeDtypeStruct((rows, model_width), jnp.bfloat16),
        in_specs=[
            pl.BlockSpec(memory_space=pltpu.SMEM),
            pl.BlockSpec(memory_space=pltpu.VMEM),
        ],
        out_specs=pl.BlockSpec(memory_space=pltpu.VMEM),
        scratch_shapes=[
            pltpu.VMEM((N_LO, 2, half, width), jnp.bfloat16),
            pltpu.VMEM((EXPERTS, half, width), jnp.bfloat16),
            pltpu.VMEM((N_HOST, half, width), jnp.bfloat16),
            dma((5,)), dma((2, N_LO, 2)), dma((N_LO, 2)), dma((N_LO, N_C)), dma((2, N_X, N_C)),
            dma((N_HOST,)), dma((N_HOST,)),
        ],
        compiler_params=pltpu.CompilerParams(
            collective_id=1, has_side_effects=True, vmem_limit_bytes=16 * 2**20
        ),
        name="weights",
    )(replica_plan, fresh)
    return (weights_next[None], first_next[None], second_next[None], replica_weight[None])


def solution(mesh):
    return jax.shard_map(
        per_device,
        mesh=mesh,
        in_specs=(
            P(None, ("dp", "expert")),
            P(("dp", "expert"), None),
            P(("dp", "expert"), None),
            P(("dp", "expert")),
            P(),
            P("expert", "dp", None),
            P("expert", "dp", None),
            P("expert", "dp", None),
        ),
        out_specs=(
            P("expert", "dp", None),
            P("expert", "dp", None),
            P("expert", "dp", None),
            P("expert", "dp", None),
        ),
        check_vma=False,
    )
```

```python
import functools

import jax
import jax.numpy as jnp
from jax import lax
from jax.experimental import pallas as pl
from jax.experimental.pallas import tpu as pltpu
from jax.sharding import PartitionSpec as P

MESH = pl.DeviceIdType.MESH

N_Y, N_X, N_C, N_LO, N_HI = 4, 4, 2, 8, 2
N_Z = N_HI * N_LO
N_HOST = N_X * N_C
QUART = 4
EXPERTS = 16
FLAG_ROWS = 16
VMEM_BYTES = 67043328
HOP_LAG = 3
STEPS = 32000.0
FINE = 65536.0
CHUNKS = ((0, 384), (384, 256))

beta_one = 0.9
beta_two = 0.95
learn_rate = 0.01
decay_rate = 0.1
epsilon = 1e-08
step_count = 10.0


def adam_update(weights, first, second, gradient):
    first_next = beta_one * first + (1.0 - beta_one) * gradient
    second_next = beta_two * second + (1.0 - beta_two) * gradient * gradient
    scaled_first = first_next / (1.0 - beta_one**step_count)
    scaled_second = second_next / (1.0 - beta_two**step_count)
    direction = scaled_first / (jnp.sqrt(scaled_second) + epsilon)
    weights_next = weights - learn_rate * (direction + decay_rate * weights)
    return (weights_next, first_next, second_next)


def place():
    g = lax.axis_index("dp")
    j = lax.axis_index("expert")
    z_hi, y = lax.div(g, N_Y), lax.rem(g, N_Y)
    z_lo, x, c = lax.div(j, N_HOST), lax.rem(lax.div(j, N_C), N_X), lax.rem(j, N_C)
    return z_hi, z_lo, y, x, c


def device(z_hi, z_lo, y, x, c):
    return (z_hi * N_Y + y, z_lo * N_HOST + x * N_C + c)


def wrap(v, n):
    return lax.rem(v + n, n)


def step_kernel(
    plan_ref, hid_ref, grad_ref, master_ref, first_ref, second_ref,
    total, out_ref,
    hall, gall, prim, repl, ring_a, ring_b, done, state, line, mixed_a, mixed_b, picked,
    own_sem, hs1, hr1, hs2, hr2, gxs, gr, gys, gyh, gcs, gcr, rs, rr, fs, fr,
    ls, lr, ms, mr, lm, ps, pr,
):
    z_hi, z_lo, y, x, c = place()
    z = z_hi * N_LO + z_lo
    rows, width = master_ref.shape
    half = rows // 2
    tok = grad_ref.shape[0]

    def here(yy, xx, cc):
        return device(z_hi, z_lo, yy, xx, cc)

    def level(zz):
        return device(lax.div(zz, N_LO), lax.rem(zz, N_LO), y, x, c)

    y_next, y_prev, y_far = wrap(y + 1, N_Y), wrap(y - 1, N_Y), wrap(y + 2, N_Y)
    partner = here(y, x, 1 - c)
    yc_peers = [
        (wrap(y + dy, N_Y), c if dc == 0 else 1 - c)
        for dy in range(N_Y) for dc in range(N_C) if (dy, dc) != (0, 0)
    ]
    x_peers = [wrap(x + dx, N_X) for dx in range(1, N_X)]
    xc_peers = [(xx, cc) for xx in x_peers for cc in (c, 1 - c)]
    me8 = y * N_C + c

    def source(yy, xx, cc):
        return (yy * N_X + xx) * N_C + cc

    me = source(y, x, c)

    def columns(q, ch):
        return pl.ds(pl.multiple_of(q * width + CHUNKS[ch][0], 128), CHUNKS[ch][1])

    def span(ch):
        return pl.ds(*CHUNKS[ch])

    own_cols = pl.ds(pl.multiple_of(x * width, 128), width)
    own_g = pltpu.make_async_copy(grad_ref.at[:, own_cols], gall.at[me], own_sem.at[0])
    own_h = pltpu.make_async_copy(hid_ref.at[c * N_Y + y], hall.at[x, me8], own_sem.at[1])
    own_h.start()
    own_g.start()
    loads = [
        pltpu.make_async_copy(ref, state.at[n], own_sem.at[2 + n])
        for n, ref in enumerate((master_ref, first_ref, second_ref))
    ]
    for copy in loads:
        copy.start()

    barrier = pltpu.get_barrier_semaphore()
    greeted = [here(yy, x, cc) for yy, cc in yc_peers] + [here(y, xx, cc) for xx, cc in xc_peers]
    greeted += [level(wrap(z + 1, N_Z)), level(wrap(z - 1, N_Z))]
    for dev in greeted:
        pl.semaphore_signal(barrier, inc=1, device_id=dev, device_id_type=MESH)
    pl.semaphore_wait(barrier, len(greeted))

    def remote(src, dst, ssem, rsem, dev):
        return pltpu.make_async_remote_copy(
            src_ref=src, dst_ref=dst, send_sem=ssem, recv_sem=rsem,
            device_id=dev, device_id_type=MESH,
        )

    def loop(first, count, body):
        def one(k, carry):
            body(k)
            return carry

        lax.fori_loop(first, first + count, one, 0)

    parts = (pl.ds(0, tok // 2), pl.ds(tok // 2, tok // 2))
    rows_of = (y, y_prev, y_next, y_far)

    def origin(group, dx):
        return rows_of[group], wrap(x - dx, N_X)

    def along_x(dx, ch):
        xx = wrap(x + dx, N_X)
        return remote(
            grad_ref.at[:, columns(xx, ch)], gall.at[me, :, span(ch)],
            gxs.at[ch, dx - 1], gr.at[ch, dx, 0], here(y, xx, c),
        )

    def along_y(way, dx, ch):
        yy, xx = origin(0, dx)
        piece = gall.at[source(yy, xx, c), :, span(ch)]
        return remote(
            piece, piece, gys.at[ch, way, dx], gr.at[ch, (1 + way) * N_X + dx, 0],
            here(y_next if way == 0 else y_prev, x, c),
        )

    def onward(way, dx, ch):
        yy, xx = origin(1 + way, dx)
        piece = gall.at[source(yy, xx, c), parts[way], span(ch)]
        return remote(
            piece, piece, gyh.at[ch, way, dx], gr.at[ch, 3 * N_X + dx, way],
            here(y_next if way == 0 else y_prev, x, c),
        )

    def across(group, dx, ch):
        yy, xx = origin(group, dx)
        piece = gall.at[source(yy, xx, c), :, span(ch)]
        return remote(piece, piece, gcs.at[ch, group, dx], gcr.at[ch, group, dx], partner)

    def arrive(group, dx, ch):
        yy, xx = origin(group, dx)
        if group < 3:
            piece = gall.at[source(yy, xx, c), :, span(ch)]
            remote(piece, piece, gys.at[ch, 0, dx], gr.at[ch, group * N_X + dx, 0], partner).wait_recv()
        else:
            for part in range(2):
                piece = gall.at[source(yy, xx, c), parts[part], span(ch)]
                remote(piece, piece, gys.at[ch, 0, dx], gr.at[ch, 3 * N_X + dx, part], partner).wait_recv()

    def spread_own(dx, ch):
        along_y(0, dx, ch).start()
        along_y(1, dx, ch).start()
        across(0, dx, ch).start()

    def take_x(dx, ch):
        arrive(0, dx, ch)
        spread_own(dx, ch)

    def take_y(dx, ch):
        for way in range(2):
            arrive(1 + way, dx, ch)
            onward(way, dx, ch).start()
            across(1 + way, dx, ch).start()

    def take_far(dx, ch):
        arrive(3, dx, ch)
        across(3, dx, ch).start()

    def add_product(yy, xx, cc, ch):
        block = hall.at[xx, yy * N_C + cc]
        product = jnp.dot(
            block[pl.ds(0, rows), :], gall[source(yy, xx, cc), :, span(ch)], preferred_element_type=jnp.float32
        )
        flag = block[pl.ds(rows, FLAG_ROWS), :].astype(jnp.float32)[0:1, :]
        flag = jnp.concatenate([jnp.broadcast_to(flag, (rows, 128))] * (CHUNKS[ch][1] // 128), axis=1)
        host = xx * N_C + cc
        rounded = product.astype(jnp.bfloat16).astype(jnp.float32)
        prim[host, :, span(ch)] += jnp.where(flag > 0.5, 0.0, product)
        repl[host, :, span(ch)] += jnp.where(flag > 0.5, rounded, 0.0)

    def rail_product(group, dx, ch):
        add_product(*origin(group, dx), c, ch)

    def take_across(k, ch):
        group, dx = lax.div(k, N_X), lax.rem(k, N_X)
        dy = jnp.where(group == 1, N_Y - 1, jnp.where(group == 2, 1, jnp.where(group == 3, 2, 0)))
        yy, xx = wrap(y + dy, N_Y), wrap(x - dx, N_X)
        piece = gall.at[source(yy, xx, 1 - c), :, span(ch)]
        remote(piece, piece, gcs.at[ch, group, dx], gcr.at[ch, group, dx], partner).wait_recv()
        add_product(yy, xx, 1 - c, ch)

    h1 = []
    for k, (yy, cc) in enumerate(yc_peers):
        h1.append(remote(hid_ref.at[cc * N_Y + yy], hall.at[x, me8], hs1.at[k], hr1.at[k], here(yy, x, cc)))
        h1[-1].start()
    for dx in range(1, N_X):
        along_x(dx, 0).start()
    own_g.wait()
    spread_own(0, 0)
    prim[...] = jnp.zeros_like(prim)
    repl[...] = jnp.zeros_like(repl)
    own_h.wait()
    for copy in h1:
        copy.wait_recv()
    h2 = []
    for k, xx in enumerate(x_peers):
        h2.append(remote(hall.at[x], hall.at[x], hs2.at[k], hr2.at[k], here(y, xx, c)))
        h2[-1].start()
    for dx in range(1, N_X):
        along_x(dx, 1).start()
    loop(1, N_X - 1, lambda dx: take_x(dx, 0))
    loop(0, N_X, lambda dx: take_y(dx, 0))
    for copy in h2:
        copy.wait_recv()
    for group in range(3):
        loop(0, N_X, lambda dx, group=group: rail_product(group, dx, 0))

    def far_first(dx):
        take_far(dx, 0)
        rail_product(3, dx, 0)

    loop(0, N_X, far_first)
    loop(0, 4 * N_X, lambda k: take_across(k, 0))

    parity = lax.rem(z_lo, 2)

    def addend(e, part, ch):
        weight = jnp.where(lax.div(e, N_HOST) == parity, 1.0, 0.0)
        total = prim[lax.rem(e, N_HOST), part, span(ch)] * weight
        for h in range(N_HOST):
            weight = jnp.where(plan_ref[z_lo * N_HOST + h] == e, 1.0, 0.0)
            total += repl[h, part, span(ch)] * weight
        return total

    offset = [wrap(z - (8 * c + 2 * x + b), N_Z) for b in range(2)]
    lag = [HOP_LAG * jnp.where(r >= 8, r - 8, jnp.where(r == 0, 8, 7 - r)) for r in offset]

    rings = (ring_a, ring_b)
    groups = half // 8
    pairs = groups // 2
    lanes = lax.shift_right_logical(lax.broadcasted_iota(jnp.int32, (8, 128), 1), 4)

    def slab(e, ch, hf, way):
        return rings[ch].at[way, e, hf]

    def encode(value, ref, ch):
        tiles = CHUNKS[ch][1] // 128
        top = jnp.zeros((8, 128), jnp.float32)
        for g in range(groups):
            top = jnp.where(lanes == g, jnp.max(jnp.abs(value[8 * g:8 * g + 8]), axis=1, keepdims=True), top)
        level_of = jnp.ceil(jnp.log2(jnp.maximum(top, 1e-30)) * FINE).astype(jnp.int32) + 64
        factor = jnp.exp2(level_of.astype(jnp.float32) * (-1.0 / FINE)) * STEPS
        whole = [
            jnp.round(value[8 * g:8 * g + 8] * factor[:, 16 * g:16 * g + 1]).astype(jnp.int32) for g in range(groups)
        ]
        for g in range(pairs):
            word = (whole[g] << 16) | (whole[g + pairs] & 0xFFFF)
            for t in range(tiles):
                ref[g * tiles + t] = word[:, 128 * t:128 * t + 128]
        ref[pairs * tiles] = level_of

    def decode(ref, ch):
        tiles = CHUNKS[ch][1] // 128
        factor = jnp.exp2(ref[pairs * tiles].astype(jnp.float32) * (1.0 / FINE)) * (1.0 / STEPS)
        upper, lower = [], []
        for g in range(pairs):
            word = jnp.concatenate([ref[g * tiles + t] for t in range(tiles)], axis=1)
            upper.append((word >> 16).astype(jnp.float32) * factor[:, 16 * g:16 * g + 1])
            k = 16 * (g + pairs)
            lower.append(((word << 16) >> 16).astype(jnp.float32) * factor[:, k:k + 1])
        return jnp.concatenate(upper + lower, axis=0)

    def hop(e, ch, hf, r):
        way = jnp.where(r >= 8, 0, 1)
        piece = slab(e, ch, hf, way)
        return remote(
            piece, piece, rs.at[ch, hf, e], rr.at[way, ch, hf, e], level(wrap(jnp.where(r >= 8, z + 1, z - 1), N_Z))
        )

    def landed(e, ch, hf, way):
        piece = slab(e, ch, hf, way)
        remote(piece, piece, rs.at[ch, hf, e], rr.at[way, ch, hf, e], partner).wait_recv()

    def deliver(e, ch, hf):
        part = pl.ds(hf * half, half)
        xx, cc = lax.rem(lax.div(e, N_C), N_X), lax.rem(e, N_C)
        return remote(
            done.at[lax.rem(e, N_HOST), part, span(ch)], total.at[part, span(ch)],
            fs.at[ch, hf, e], fr.at[ch, hf], here(y, xx, cc),
        )

    def keep(e, ch, hf):
        part = pl.ds(hf * half, half)
        return pltpu.make_async_copy(
            done.at[lax.rem(e, N_HOST), part, span(ch)], total.at[part, span(ch)], fr.at[ch, hf]
        )

    def mine(e):
        return lax.rem(e, N_HOST) == x * N_C + c

    def unit(e, ch, r):
        for hf in range(2):
            part = pl.ds(hf * half, half)
            way = jnp.where(r >= 8, 0, 1)

            @pl.when((r == 7) | (r == 8))
            def _():
                encode(addend(e, part, ch), slab(e, ch, hf, way), ch)

            @pl.when((r != 7) & (r != 8) & (r != 0))
            def _():
                own = addend(e, part, ch)
                landed(e, ch, hf, way)
                encode(own + decode(slab(e, ch, hf, way), ch), slab(e, ch, hf, way), ch)

            @pl.when(r != 0)
            def _():
                hop(e, ch, hf, r).start()

            @pl.when(r == 0)
            def _():
                own = addend(e, part, ch)
                landed(e, ch, hf, 0)
                landed(e, ch, hf, 1)
                done[lax.rem(e, N_HOST), part, span(ch)] = (
                    own + decode(slab(e, ch, hf, 0), ch) + decode(slab(e, ch, hf, 1), ch)
                )

                @pl.when(mine(e))
                def _():
                    keep(e, ch, hf).start()

                @pl.when(jnp.logical_not(mine(e)))
                def _():
                    deliver(e, ch, hf).start()

    def units(i):
        for ch in range(2):
            for b in range(2):
                first = EXPERTS * ch + N_HOST * b
                n = i - lag[b]

                @pl.when((n >= first) & (n < first + N_HOST))
                def _():
                    unit(n - EXPERTS * ch, ch, offset[b])

    kept = (x == lax.div(z_lo, 2)) & (c == z_hi)
    e_own = parity * N_HOST + x * N_C + c

    def adam(ch):
        for hf in range(2):
            @pl.when(kept)
            def _():
                keep(e_own, ch, hf).wait()

            @pl.when(jnp.logical_not(kept))
            def _():
                deliver(e_own, ch, hf).wait_recv()

            part = pl.ds(hf * half, half)
            weights_next = adam_update(
                state[0, part, span(ch)], state[1, part, span(ch)], state[2, part, span(ch)], total[part, span(ch)]
            )[0]
            line[z_lo, hf, :, span(ch)] = weights_next.astype(jnp.bfloat16)

    def line_copy(d, k, hf, ch):
        piece = line.at[k, hf, :, span(ch)]
        dev = level(wrap(z + 1, N_Z) if d == 0 else wrap(z - 1, N_Z))
        return remote(piece, piece, ls.at[ch, d, k, hf], lr.at[ch, k, hf], dev)

    mixed = (mixed_a, mixed_b)

    def mix_copy(k, cc, ch):
        q, b = lax.div(k, 2), lax.rem(k, 2)
        e = b * N_HOST + x * N_C + c
        dist = wrap(q - x, N_X)
        apart = jnp.where(cc == c, 0, 1)
        return remote(
            line.at[k, cc, :, span(ch)], mixed[ch].at[e], ms.at[ch, k, cc], mr.at[ch, b, dist, apart],
            here(y, q, cc),
        )

    def local_mix(k, ch):
        b = lax.rem(k, 2)
        return pltpu.make_async_copy(
            line.at[k, c, :, span(ch)], mixed[ch].at[b * N_HOST + x * N_C + c], lm.at[ch, b]
        )

    def scatter(k, cc, ch):
        same = (lax.div(k, 2) == x) & (cc == c)

        @pl.when(same)
        def _():
            local_mix(k, ch).start()

        @pl.when(jnp.logical_not(same))
        def _():
            mix_copy(k, cc, ch).start()

    def line_start(ch):
        for hf in range(2):
            @pl.when(z_lo < N_LO - 1)
            def _():
                line_copy(0, z_lo, hf, ch).start()

            @pl.when(z_lo > 0)
            def _():
                line_copy(1, z_lo, hf, ch).start()

        for hf in range(2):
            scatter(z_lo, hf, ch)

    def line_step(t, ch):
        k, k2 = z_lo - t, z_lo + t
        for hf in range(2):
            @pl.when(k >= 0)
            def _():
                line_copy(0, k, hf, ch).wait_recv()

                @pl.when(z_lo < N_LO - 1)
                def _():
                    line_copy(0, k, hf, ch).start()

                scatter(k, hf, ch)

            @pl.when(k2 < N_LO)
            def _():
                line_copy(1, k2, hf, ch).wait_recv()

                @pl.when(z_lo > 0)
                def _():
                    line_copy(1, k2, hf, ch).start()

                scatter(k2, hf, ch)

    plane = [(dx, dc) for dx in range(N_X) for dc in range(N_C)]

    def pick_copy(n, ch):
        dx, dc = plane[n]
        target = out_ref.at[pl.ds(pl.multiple_of(c * half, 16), half), columns(x, ch)]
        piece = picked.at[n, :, span(ch)]
        if n == 0:
            return pltpu.make_async_copy(piece, target, pr.at[ch, 0])
        return remote(piece, target, ps.at[ch, n], pr.at[ch, n], here(y, wrap(x + dx, N_X), c if dc == 0 else 1 - c))

    def pick(ch):
        for b in range(2):
            local_mix(2 * x + b, ch).wait()
            for dx, dc in plane[1:]:
                piece = mixed[ch].at[0]
                remote(piece, piece, ms.at[ch, 0, 0], mr.at[ch, b, dx, dc], partner).wait_recv()
        for n, (dx, dc) in enumerate(plane):
            xx, cc = wrap(x + dx, N_X), (c if dc == 0 else 1 - c)
            picked[n, :, span(ch)] = mixed[ch][plan_ref[z_lo * N_HOST + xx * N_C + cc]]
            pick_copy(n, ch).start()


    def step_x(i):
        @pl.when(i > 0)
        def _():
            arrive(0, i, 1)

        spread_own(i, 1)
        rail_product(0, i, 1)
        units(i)

    def step_y(i):
        take_y(i - 4, 1)
        rail_product(1, i - 4, 1)
        rail_product(2, i - 4, 1)
        units(i)

    def step_far(i):
        take_far(i - 8, 1)
        rail_product(3, i - 8, 1)
        units(i)

    def step_across(i):
        loop(4 * (i - 12), 4, lambda k: take_across(k, 1))
        units(i)

    for first, step in ((0, step_x), (4, step_y), (8, step_far), (12, step_across)):
        loop(first, 4, step)
    filled = 8 * HOP_LAG
    loop(16, filled, units)
    for copy in loads:
        copy.wait()
    adam(0)
    line_start(0)

    def step_line(t):
        units(filled + 14 + 2 * t)
        line_step(t, 0)
        units(filled + 15 + 2 * t)

    loop(1, N_LO - 1, step_line)
    loop(filled + 30, 2, units)
    adam(1)
    line_start(1)
    line_step(1, 1)
    pick(0)
    loop(2, N_LO - 2, lambda t: line_step(t, 1))
    pick(1)

    for copy in h1 + h2:
        copy.wait_send()
    for ch in range(2):
        def drain(dx, ch=ch):
            for way in range(2):
                along_y(way, dx, ch).wait_send()
                onward(way, dx, ch).wait_send()
            for group in range(4):
                across(group, dx, ch).wait_send()

        for dx in range(1, N_X):
            along_x(dx, ch).wait_send()
        loop(0, N_X, drain)

        def drain_units(e, ch=ch):
            b = lax.div(e, N_HOST)
            r = jnp.where(b == 0, offset[0], offset[1])
            for hf in range(2):
                @pl.when(r != 0)
                def _():
                    hop(e, ch, hf, r).wait_send()

                @pl.when((r == 0) & jnp.logical_not(mine(e)))
                def _():
                    deliver(e, ch, hf).wait_send()

        loop(0, EXPERTS, drain_units)
    for ch in range(2):
        def drain_line(k, ch=ch):
            for hf in range(2):
                @pl.when((z_lo < N_LO - 1) & (k <= z_lo))
                def _():
                    line_copy(0, k, hf, ch).wait_send()

                @pl.when((z_lo > 0) & (k >= z_lo))
                def _():
                    line_copy(1, k, hf, ch).wait_send()

                @pl.when(jnp.logical_not((lax.div(k, 2) == x) & (hf == c)))
                def _():
                    mix_copy(k, hf, ch).wait_send()

        loop(0, N_LO, drain_line)
        for n in range(N_HOST):
            pick_copy(n, ch).wait()


def per_device(
    hidden_rows, grad_rows, block_slot, live_rows, replica_plan, master, moment_one, moment_two
):
    hidden_units, tok = hidden_rows.shape
    model_width = grad_rows.shape[1]
    groups = N_HI * N_Y
    rows = hidden_units // groups
    width = model_width // QUART
    half = rows // 2
    kept = lax.iota(jnp.int32, tok) < live_rows[0]
    masked = jnp.where(kept[None, :], hidden_rows, jnp.zeros_like(hidden_rows)).reshape(groups, rows, tok)
    flags = jnp.broadcast_to((block_slot[0, 0] == 1).astype(jnp.bfloat16), (groups, FLAG_ROWS, tok))
    hid = jnp.concatenate([masked, flags], axis=1)
    dma = pltpu.SemaphoreType.DMA
    share = jax.ShapeDtypeStruct((rows, width), jnp.float32)
    hbm, vmem = pl.BlockSpec(memory_space=pltpu.HBM), pl.BlockSpec(memory_space=pltpu.VMEM)
    gradient, replica_weight = pl.pallas_call(
        step_kernel,
        out_shape=(share, jax.ShapeDtypeStruct((rows, model_width), jnp.bfloat16)),
        in_specs=[pl.BlockSpec(memory_space=pltpu.SMEM)] + [hbm] * 5,
        out_specs=(vmem,) * 2,
        scratch_shapes=[
            pltpu.VMEM((N_X, N_Y * N_C, rows + FLAG_ROWS, tok), jnp.bfloat16),
            pltpu.VMEM((N_Y * N_X * N_C, tok, width), jnp.bfloat16),
            pltpu.VMEM((N_HOST, rows, width), jnp.float32),
            pltpu.VMEM((N_HOST, rows, width), jnp.float32),
            pltpu.VMEM((2, EXPERTS, 2, half // 16 * (CHUNKS[0][1] // 128) + 1, 8, 128), jnp.int32),
            pltpu.VMEM((2, EXPERTS, 2, half // 16 * (CHUNKS[1][1] // 128) + 1, 8, 128), jnp.int32),
            pltpu.VMEM((N_HOST, rows, width), jnp.float32),
            pltpu.VMEM((3, rows, width), jnp.float32),
            pltpu.VMEM((N_LO, 2, half, width), jnp.bfloat16),
            pltpu.VMEM((EXPERTS, half, CHUNKS[0][1]), jnp.bfloat16),
            pltpu.VMEM((EXPERTS, half, CHUNKS[1][1]), jnp.bfloat16),
            pltpu.VMEM((N_HOST, half, width), jnp.bfloat16),
            dma((5,)), dma((7,)), dma((7,)), dma((3,)), dma((3,)),
            dma((2, 3)), dma((2, 4 * N_X, 2)), dma((2, 2, N_X)), dma((2, 2, N_X)), dma((2, 4, N_X)), dma((2, 4, N_X)),
            dma((2, 2, EXPERTS)), dma((2, 2, 2, EXPERTS)), dma((2, 2, EXPERTS)), dma((2, 2)),
            dma((2, 2, N_LO, 2)), dma((2, N_LO, 2)), dma((2, N_LO, N_C)), dma((2, 2, N_X, N_C)), dma((2, 2)),
            dma((2, N_HOST)), dma((2, N_HOST)),
        ],
        compiler_params=pltpu.CompilerParams(
            collective_id=0, has_side_effects=True, vmem_limit_bytes=VMEM_BYTES
        ),
        name="step",
    )(replica_plan, hid, grad_rows, master[0], moment_one[0], moment_two[0])
    weights_next, first_next, second_next = adam_update(master[0], moment_one[0], moment_two[0], gradient)
    return (weights_next[None], first_next[None], second_next[None], replica_weight[None])


def solution(mesh):
    return jax.shard_map(
        per_device,
        mesh=mesh,
        in_specs=(
            P(None, ("dp", "expert")),
            P(("dp", "expert"), None),
            P(("dp", "expert"), None),
            P(("dp", "expert")),
            P(),
            P("expert", "dp", None),
            P("expert", "dp", None),
            P("expert", "dp", None),
        ),
        out_specs=(
            P("expert", "dp", None),
            P("expert", "dp", None),
            P("expert", "dp", None),
            P("expert", "dp", None),
        ),
        check_vma=False,
    )
```

```python
import functools

import jax
import jax.numpy as jnp
from jax import lax
from jax.experimental import pallas as pl
from jax.experimental.pallas import tpu as pltpu
from jax.sharding import PartitionSpec as P

MESH = pl.DeviceIdType.MESH

N_Y, N_X, N_C, N_LO, N_HI = 4, 4, 2, 8, 2
N_Z = N_HI * N_LO
N_HOST = N_X * N_C
QUART = 4
EXPERTS = 16
FLAG_ROWS = 16
VMEM_BYTES = 67043328
HOP_LAG = 4
STEPS = 32000.0
FINE = 65536.0
CHUNKS = ((0, 384), (384, 256))

beta_one = 0.9
beta_two = 0.95
learn_rate = 0.01
decay_rate = 0.1
epsilon = 1e-08
step_count = 10.0


def adam_update(weights, first, second, gradient):
    first_next = beta_one * first + (1.0 - beta_one) * gradient
    second_next = beta_two * second + (1.0 - beta_two) * gradient * gradient
    scaled_first = first_next / (1.0 - beta_one**step_count)
    scaled_second = second_next / (1.0 - beta_two**step_count)
    direction = scaled_first / (jnp.sqrt(scaled_second) + epsilon)
    weights_next = weights - learn_rate * (direction + decay_rate * weights)
    return (weights_next, first_next, second_next)


def place():
    g = lax.axis_index("dp")
    j = lax.axis_index("expert")
    z_hi, y = lax.div(g, N_Y), lax.rem(g, N_Y)
    z_lo, x, c = lax.div(j, N_HOST), lax.rem(lax.div(j, N_C), N_X), lax.rem(j, N_C)
    return z_hi, z_lo, y, x, c


def device(z_hi, z_lo, y, x, c):
    return (z_hi * N_Y + y, z_lo * N_HOST + x * N_C + c)


def wrap(v, n):
    return lax.rem(v + n, n)


def step_kernel(
    plan_ref, hid_ref, grad_ref, master_ref, first_ref, second_ref,
    total, out_ref,
    hall, gall, prim, repl, ring_a, ring_b, done, state, line, mixed_a, mixed_b, picked,
    own_sem, hs1, hr1, hs2, hr2, gxs, gr, gys, gyh, gcs, gcr, rs, rr, fs, fr,
    ls, lr, ms, mr, lm, ps, pr,
):
    z_hi, z_lo, y, x, c = place()
    z = z_hi * N_LO + z_lo
    rows, width = master_ref.shape
    half = rows // 2
    tok = grad_ref.shape[0]

    def here(yy, xx, cc):
        return device(z_hi, z_lo, yy, xx, cc)

    def level(zz):
        return device(lax.div(zz, N_LO), lax.rem(zz, N_LO), y, x, c)

    y_next, y_prev, y_far = wrap(y + 1, N_Y), wrap(y - 1, N_Y), wrap(y + 2, N_Y)
    partner = here(y, x, 1 - c)
    yc_peers = [
        (wrap(y + dy, N_Y), c if dc == 0 else 1 - c)
        for dy in range(N_Y) for dc in range(N_C) if (dy, dc) != (0, 0)
    ]
    x_peers = [wrap(x + dx, N_X) for dx in range(1, N_X)]
    xc_peers = [(xx, cc) for xx in x_peers for cc in (c, 1 - c)]
    me8 = y * N_C + c

    def source(yy, xx, cc):
        return (yy * N_X + xx) * N_C + cc

    me = source(y, x, c)

    def columns(q, ch):
        return pl.ds(pl.multiple_of(q * width + CHUNKS[ch][0], 128), CHUNKS[ch][1])

    def span(ch):
        return pl.ds(*CHUNKS[ch])

    own_cols = pl.ds(pl.multiple_of(x * width, 128), width)
    own_g = pltpu.make_async_copy(grad_ref.at[:, own_cols], gall.at[me], own_sem.at[0])
    own_h = pltpu.make_async_copy(hid_ref.at[c * N_Y + y], hall.at[x, me8], own_sem.at[1])
    own_h.start()
    own_g.start()
    loads = [
        pltpu.make_async_copy(ref, state.at[n], own_sem.at[2 + n])
        for n, ref in enumerate((master_ref, first_ref, second_ref))
    ]
    for copy in loads:
        copy.start()

    barrier = pltpu.get_barrier_semaphore()
    greeted = [here(yy, x, cc) for yy, cc in yc_peers] + [here(y, xx, cc) for xx, cc in xc_peers]
    greeted += [level(wrap(z + 1, N_Z)), level(wrap(z - 1, N_Z))]
    for dev in greeted:
        pl.semaphore_signal(barrier, inc=1, device_id=dev, device_id_type=MESH)
    pl.semaphore_wait(barrier, len(greeted))

    def remote(src, dst, ssem, rsem, dev):
        return pltpu.make_async_remote_copy(
            src_ref=src, dst_ref=dst, send_sem=ssem, recv_sem=rsem,
            device_id=dev, device_id_type=MESH,
        )

    def loop(first, count, body):
        def one(k, carry):
            body(k)
            return carry

        lax.fori_loop(first, first + count, one, 0)

    parts = (pl.ds(0, tok // 2), pl.ds(tok // 2, tok // 2))
    rows_of = (y, y_prev, y_next, y_far)

    def origin(group, dx):
        return rows_of[group], wrap(x - dx, N_X)

    def along_x(dx, ch):
        xx = wrap(x + dx, N_X)
        return remote(
            grad_ref.at[:, columns(xx, ch)], gall.at[me, :, span(ch)],
            gxs.at[ch, dx - 1], gr.at[ch, dx, 0], here(y, xx, c),
        )

    def along_y(way, dx, ch):
        yy, xx = origin(0, dx)
        piece = gall.at[source(yy, xx, c), :, span(ch)]
        return remote(
            piece, piece, gys.at[ch, way, dx], gr.at[ch, (1 + way) * N_X + dx, 0],
            here(y_next if way == 0 else y_prev, x, c),
        )

    def onward(way, dx, ch):
        yy, xx = origin(1 + way, dx)
        piece = gall.at[source(yy, xx, c), parts[way], span(ch)]
        return remote(
            piece, piece, gyh.at[ch, way, dx], gr.at[ch, 3 * N_X + dx, way],
            here(y_next if way == 0 else y_prev, x, c),
        )

    def across(group, dx, ch):
        yy, xx = origin(group, dx)
        piece = gall.at[source(yy, xx, c), :, span(ch)]
        return remote(piece, piece, gcs.at[ch, group, dx], gcr.at[ch, group, dx], partner)

    def arrive(group, dx, ch):
        yy, xx = origin(group, dx)
        if group < 3:
            piece = gall.at[source(yy, xx, c), :, span(ch)]
            remote(piece, piece, gys.at[ch, 0, dx], gr.at[ch, group * N_X + dx, 0], partner).wait_recv()
        else:
            for part in range(2):
                piece = gall.at[source(yy, xx, c), parts[part], span(ch)]
                remote(piece, piece, gys.at[ch, 0, dx], gr.at[ch, 3 * N_X + dx, part], partner).wait_recv()

    def spread_own(dx, ch):
        along_y(0, dx, ch).start()
        along_y(1, dx, ch).start()
        across(0, dx, ch).start()

    def take_x(dx, ch):
        arrive(0, dx, ch)
        spread_own(dx, ch)

    def take_y(dx, ch):
        for way in range(2):
            arrive(1 + way, dx, ch)
            onward(way, dx, ch).start()
            across(1 + way, dx, ch).start()

    def take_far(dx, ch):
        arrive(3, dx, ch)
        across(3, dx, ch).start()

    def add_product(yy, xx, cc, ch):
        block = hall.at[xx, yy * N_C + cc]
        product = jnp.dot(
            block[pl.ds(0, rows), :], gall[source(yy, xx, cc), :, span(ch)], preferred_element_type=jnp.float32
        )
        flag = block[pl.ds(rows, FLAG_ROWS), :].astype(jnp.float32)[0:1, :]
        flag = jnp.concatenate([jnp.broadcast_to(flag, (rows, 128))] * (CHUNKS[ch][1] // 128), axis=1)
        host = xx * N_C + cc
        rounded = product.astype(jnp.bfloat16).astype(jnp.float32)
        prim[host, :, span(ch)] += jnp.where(flag > 0.5, 0.0, product)
        repl[host, :, span(ch)] += jnp.where(flag > 0.5, rounded, 0.0)

    def rail_product(group, dx, ch):
        add_product(*origin(group, dx), c, ch)

    def take_across(k, ch):
        group, dx = lax.div(k, N_X), lax.rem(k, N_X)
        dy = jnp.where(group == 1, N_Y - 1, jnp.where(group == 2, 1, jnp.where(group == 3, 2, 0)))
        yy, xx = wrap(y + dy, N_Y), wrap(x - dx, N_X)
        piece = gall.at[source(yy, xx, 1 - c), :, span(ch)]
        remote(piece, piece, gcs.at[ch, group, dx], gcr.at[ch, group, dx], partner).wait_recv()
        add_product(yy, xx, 1 - c, ch)

    h1 = []
    for k, (yy, cc) in enumerate(yc_peers):
        h1.append(remote(hid_ref.at[cc * N_Y + yy], hall.at[x, me8], hs1.at[k], hr1.at[k], here(yy, x, cc)))
        h1[-1].start()
    for dx in range(1, N_X):
        along_x(dx, 0).start()
    own_g.wait()
    spread_own(0, 0)
    prim[...] = jnp.zeros_like(prim)
    repl[...] = jnp.zeros_like(repl)
    own_h.wait()
    for copy in h1:
        copy.wait_recv()
    h2 = []
    for k, xx in enumerate(x_peers):
        h2.append(remote(hall.at[x], hall.at[x], hs2.at[k], hr2.at[k], here(y, xx, c)))
        h2[-1].start()
    for dx in range(1, N_X):
        along_x(dx, 1).start()
    def nearest(k):
        return jnp.where(k == 2, 3, jnp.where(k == 3, 2, k))

    loop(1, N_X - 1, lambda k: take_x(nearest(k), 0))
    loop(0, N_X, lambda k: take_y(nearest(k), 0))
    for copy in h2:
        copy.wait_recv()
    for group in range(3):
        loop(0, N_X, lambda dx, group=group: rail_product(group, dx, 0))

    def far_first(dx):
        take_far(dx, 0)
        rail_product(3, dx, 0)

    loop(0, N_X, far_first)
    loop(0, 4 * N_X, lambda k: take_across(k, 0))

    parity = lax.rem(z_lo, 2)

    def addend(e, part, ch):
        weight = jnp.where(lax.div(e, N_HOST) == parity, 1.0, 0.0)
        total = prim[lax.rem(e, N_HOST), part, span(ch)] * weight
        for h in range(N_HOST):
            weight = jnp.where(plan_ref[z_lo * N_HOST + h] == e, 1.0, 0.0)
            total += repl[h, part, span(ch)] * weight
        return total

    offset = [wrap(z - (8 * c + 2 * x + b), N_Z) for b in range(2)]
    lag = [HOP_LAG * jnp.where(r >= 8, r - 8, jnp.where(r == 0, 8, 7 - r)) for r in offset]

    rings = (ring_a, ring_b)
    groups = half // 8
    pairs = groups // 2
    lanes = lax.shift_right_logical(lax.broadcasted_iota(jnp.int32, (8, 128), 1), 4)

    def slab(e, ch, hf, way):
        return rings[ch].at[way, e, hf]

    def encode(value, ref, ch):
        tiles = CHUNKS[ch][1] // 128
        top = jnp.zeros((8, 128), jnp.float32)
        for g in range(groups):
            top = jnp.where(lanes == g, jnp.max(jnp.abs(value[8 * g:8 * g + 8]), axis=1, keepdims=True), top)
        level_of = jnp.ceil(jnp.log2(jnp.maximum(top, 1e-30)) * FINE).astype(jnp.int32) + 64
        factor = jnp.exp2(level_of.astype(jnp.float32) * (-1.0 / FINE)) * STEPS
        whole = [
            jnp.round(value[8 * g:8 * g + 8] * factor[:, 16 * g:16 * g + 1]).astype(jnp.int32) for g in range(groups)
        ]
        for g in range(pairs):
            word = (whole[g] << 16) | (whole[g + pairs] & 0xFFFF)
            for t in range(tiles):
                ref[g * tiles + t] = word[:, 128 * t:128 * t + 128]
        ref[pairs * tiles] = level_of

    def decode(ref, ch):
        tiles = CHUNKS[ch][1] // 128
        factor = jnp.exp2(ref[pairs * tiles].astype(jnp.float32) * (1.0 / FINE)) * (1.0 / STEPS)
        upper, lower = [], []
        for g in range(pairs):
            word = jnp.concatenate([ref[g * tiles + t] for t in range(tiles)], axis=1)
            upper.append((word >> 16).astype(jnp.float32) * factor[:, 16 * g:16 * g + 1])
            k = 16 * (g + pairs)
            lower.append(((word << 16) >> 16).astype(jnp.float32) * factor[:, k:k + 1])
        return jnp.concatenate(upper + lower, axis=0)

    def hop(e, ch, hf, r):
        way = jnp.where(r >= 8, 0, 1)
        piece = slab(e, ch, hf, way)
        return remote(
            piece, piece, rs.at[ch, hf, e], rr.at[way, ch, hf, e], level(wrap(jnp.where(r >= 8, z + 1, z - 1), N_Z))
        )

    def landed(e, ch, hf, way):
        piece = slab(e, ch, hf, way)
        remote(piece, piece, rs.at[ch, hf, e], rr.at[way, ch, hf, e], partner).wait_recv()

    def deliver(e, ch, hf):
        part = pl.ds(hf * half, half)
        xx, cc = lax.rem(lax.div(e, N_C), N_X), lax.rem(e, N_C)
        return remote(
            done.at[lax.rem(e, N_HOST), part, span(ch)], total.at[part, span(ch)],
            fs.at[ch, hf, e], fr.at[ch, hf], here(y, xx, cc),
        )

    def keep(e, ch, hf):
        part = pl.ds(hf * half, half)
        return pltpu.make_async_copy(
            done.at[lax.rem(e, N_HOST), part, span(ch)], total.at[part, span(ch)], fr.at[ch, hf]
        )

    def mine(e):
        return lax.rem(e, N_HOST) == x * N_C + c

    def unit(e, ch, r):
        for hf in range(2):
            part = pl.ds(hf * half, half)
            way = jnp.where(r >= 8, 0, 1)

            @pl.when((r == 7) | (r == 8))
            def _():
                encode(addend(e, part, ch), slab(e, ch, hf, way), ch)

            @pl.when((r != 7) & (r != 8) & (r != 0))
            def _():
                own = addend(e, part, ch)
                landed(e, ch, hf, way)
                encode(own + decode(slab(e, ch, hf, way), ch), slab(e, ch, hf, way), ch)

            @pl.when(r != 0)
            def _():
                hop(e, ch, hf, r).start()

            @pl.when(r == 0)
            def _():
                own = addend(e, part, ch)
                landed(e, ch, hf, 0)
                landed(e, ch, hf, 1)
                done[lax.rem(e, N_HOST), part, span(ch)] = (
                    own + decode(slab(e, ch, hf, 0), ch) + decode(slab(e, ch, hf, 1), ch)
                )

                @pl.when(mine(e))
                def _():
                    keep(e, ch, hf).start()

                @pl.when(jnp.logical_not(mine(e)))
                def _():
                    deliver(e, ch, hf).start()

    def units(i):
        for ch in range(2):
            for b in range(2):
                first = EXPERTS * ch + N_HOST * b
                n = i - lag[b]

                @pl.when((n >= first) & (n < first + N_HOST))
                def _():
                    unit(n - EXPERTS * ch, ch, offset[b])

    kept = (x == lax.div(z_lo, 2)) & (c == z_hi)
    e_own = parity * N_HOST + x * N_C + c

    def adam(ch):
        for hf in range(2):
            @pl.when(kept)
            def _():
                keep(e_own, ch, hf).wait()

            @pl.when(jnp.logical_not(kept))
            def _():
                deliver(e_own, ch, hf).wait_recv()

            part = pl.ds(hf * half, half)
            weights_next = adam_update(
                state[0, part, span(ch)], state[1, part, span(ch)], state[2, part, span(ch)], total[part, span(ch)]
            )[0]
            line[z_lo, hf, :, span(ch)] = weights_next.astype(jnp.bfloat16)

    def line_copy(d, k, hf, ch):
        piece = line.at[k, hf, :, span(ch)]
        dev = level(wrap(z + 1, N_Z) if d == 0 else wrap(z - 1, N_Z))
        return remote(piece, piece, ls.at[ch, d, k, hf], lr.at[ch, k, hf], dev)

    mixed = (mixed_a, mixed_b)

    def mix_copy(k, cc, ch):
        q, b = lax.div(k, 2), lax.rem(k, 2)
        e = b * N_HOST + x * N_C + c
        dist = wrap(q - x, N_X)
        apart = jnp.where(cc == c, 0, 1)
        return remote(
            line.at[k, cc, :, span(ch)], mixed[ch].at[e], ms.at[ch, k, cc], mr.at[ch, b, dist, apart],
            here(y, q, cc),
        )

    def local_mix(k, ch):
        b = lax.rem(k, 2)
        return pltpu.make_async_copy(
            line.at[k, c, :, span(ch)], mixed[ch].at[b * N_HOST + x * N_C + c], lm.at[ch, b]
        )

    def scatter(k, cc, ch):
        same = (lax.div(k, 2) == x) & (cc == c)

        @pl.when(same)
        def _():
            local_mix(k, ch).start()

        @pl.when(jnp.logical_not(same))
        def _():
            mix_copy(k, cc, ch).start()

    def line_start(ch):
        for hf in range(2):
            @pl.when(z_lo < N_LO - 1)
            def _():
                line_copy(0, z_lo, hf, ch).start()

            @pl.when(z_lo > 0)
            def _():
                line_copy(1, z_lo, hf, ch).start()

        for hf in range(2):
            scatter(z_lo, hf, ch)

    def line_step(t, ch):
        k, k2 = z_lo - t, z_lo + t
        for hf in range(2):
            @pl.when(k >= 0)
            def _():
                line_copy(0, k, hf, ch).wait_recv()

                @pl.when(z_lo < N_LO - 1)
                def _():
                    line_copy(0, k, hf, ch).start()

                scatter(k, hf, ch)

            @pl.when(k2 < N_LO)
            def _():
                line_copy(1, k2, hf, ch).wait_recv()

                @pl.when(z_lo > 0)
                def _():
                    line_copy(1, k2, hf, ch).start()

                scatter(k2, hf, ch)

    plane = [(dx, dc) for dx in range(N_X) for dc in range(N_C)]

    def pick_copy(n, ch):
        dx, dc = plane[n]
        target = out_ref.at[pl.ds(pl.multiple_of(c * half, 16), half), columns(x, ch)]
        piece = picked.at[n, :, span(ch)]
        if n == 0:
            return pltpu.make_async_copy(piece, target, pr.at[ch, 0])
        return remote(piece, target, ps.at[ch, n], pr.at[ch, n], here(y, wrap(x + dx, N_X), c if dc == 0 else 1 - c))

    def pick(ch):
        for b in range(2):
            local_mix(2 * x + b, ch).wait()
            for dx, dc in plane[1:]:
                piece = mixed[ch].at[0]
                remote(piece, piece, ms.at[ch, 0, 0], mr.at[ch, b, dx, dc], partner).wait_recv()
        for n, (dx, dc) in enumerate(plane):
            xx, cc = wrap(x + dx, N_X), (c if dc == 0 else 1 - c)
            picked[n, :, span(ch)] = mixed[ch][plan_ref[z_lo * N_HOST + xx * N_C + cc]]
            pick_copy(n, ch).start()


    def step_x(i):
        @pl.when(i > 0)
        def _():
            arrive(0, i, 1)

        spread_own(i, 1)
        rail_product(0, i, 1)
        units(i)

    def step_y(i):
        take_y(i - 4, 1)
        rail_product(1, i - 4, 1)
        rail_product(2, i - 4, 1)
        units(i)

    def step_far(i):
        take_far(i - 8, 1)
        rail_product(3, i - 8, 1)
        units(i)

    def step_across(i):
        loop(4 * (i - 12), 4, lambda k: take_across(k, 1))
        units(i)

    for first, step in ((0, step_x), (4, step_y), (8, step_far), (12, step_across)):
        loop(first, 4, step)
    filled = 8 * HOP_LAG
    loop(16, filled, units)
    for copy in loads:
        copy.wait()
    adam(0)
    line_start(0)

    def step_line(t):
        units(filled + 14 + 2 * t)
        line_step(t, 0)
        units(filled + 15 + 2 * t)

    loop(1, N_LO - 1, step_line)
    loop(filled + 30, 2, units)
    adam(1)
    line_start(1)
    line_step(1, 1)
    pick(0)
    loop(2, N_LO - 2, lambda t: line_step(t, 1))
    pick(1)

    for copy in h1 + h2:
        copy.wait_send()
    for ch in range(2):
        def drain(dx, ch=ch):
            for way in range(2):
                along_y(way, dx, ch).wait_send()
                onward(way, dx, ch).wait_send()
            for group in range(4):
                across(group, dx, ch).wait_send()

        for dx in range(1, N_X):
            along_x(dx, ch).wait_send()
        loop(0, N_X, drain)

        def drain_units(e, ch=ch):
            b = lax.div(e, N_HOST)
            r = jnp.where(b == 0, offset[0], offset[1])
            for hf in range(2):
                @pl.when(r != 0)
                def _():
                    hop(e, ch, hf, r).wait_send()

                @pl.when((r == 0) & jnp.logical_not(mine(e)))
                def _():
                    deliver(e, ch, hf).wait_send()

        loop(0, EXPERTS, drain_units)
    for ch in range(2):
        def drain_line(k, ch=ch):
            for hf in range(2):
                @pl.when((z_lo < N_LO - 1) & (k <= z_lo))
                def _():
                    line_copy(0, k, hf, ch).wait_send()

                @pl.when((z_lo > 0) & (k >= z_lo))
                def _():
                    line_copy(1, k, hf, ch).wait_send()

                @pl.when(jnp.logical_not((lax.div(k, 2) == x) & (hf == c)))
                def _():
                    mix_copy(k, hf, ch).wait_send()

        loop(0, N_LO, drain_line)
        for n in range(N_HOST):
            pick_copy(n, ch).wait()


def per_device(
    hidden_rows, grad_rows, block_slot, live_rows, replica_plan, master, moment_one, moment_two
):
    hidden_units, tok = hidden_rows.shape
    model_width = grad_rows.shape[1]
    groups = N_HI * N_Y
    rows = hidden_units // groups
    width = model_width // QUART
    half = rows // 2
    kept = lax.iota(jnp.int32, tok) < live_rows[0]
    masked = jnp.where(kept[None, :], hidden_rows, jnp.zeros_like(hidden_rows)).reshape(groups, rows, tok)
    flags = jnp.broadcast_to((block_slot[0, 0] == 1).astype(jnp.bfloat16), (groups, FLAG_ROWS, tok))
    hid = jnp.concatenate([masked, flags], axis=1)
    dma = pltpu.SemaphoreType.DMA
    share = jax.ShapeDtypeStruct((rows, width), jnp.float32)
    hbm, vmem = pl.BlockSpec(memory_space=pltpu.HBM), pl.BlockSpec(memory_space=pltpu.VMEM)
    gradient, replica_weight = pl.pallas_call(
        step_kernel,
        out_shape=(share, jax.ShapeDtypeStruct((rows, model_width), jnp.bfloat16)),
        in_specs=[pl.BlockSpec(memory_space=pltpu.SMEM)] + [hbm] * 5,
        out_specs=(vmem,) * 2,
        scratch_shapes=[
            pltpu.VMEM((N_X, N_Y * N_C, rows + FLAG_ROWS, tok), jnp.bfloat16),
            pltpu.VMEM((N_Y * N_X * N_C, tok, width), jnp.bfloat16),
            pltpu.VMEM((N_HOST, rows, width), jnp.float32),
            pltpu.VMEM((N_HOST, rows, width), jnp.float32),
            pltpu.VMEM((2, EXPERTS, 2, half // 16 * (CHUNKS[0][1] // 128) + 1, 8, 128), jnp.int32),
            pltpu.VMEM((2, EXPERTS, 2, half // 16 * (CHUNKS[1][1] // 128) + 1, 8, 128), jnp.int32),
            pltpu.VMEM((N_HOST, rows, width), jnp.float32),
            pltpu.VMEM((3, rows, width), jnp.float32),
            pltpu.VMEM((N_LO, 2, half, width), jnp.bfloat16),
            pltpu.VMEM((EXPERTS, half, CHUNKS[0][1]), jnp.bfloat16),
            pltpu.VMEM((EXPERTS, half, CHUNKS[1][1]), jnp.bfloat16),
            pltpu.VMEM((N_HOST, half, width), jnp.bfloat16),
            dma((5,)), dma((7,)), dma((7,)), dma((3,)), dma((3,)),
            dma((2, 3)), dma((2, 4 * N_X, 2)), dma((2, 2, N_X)), dma((2, 2, N_X)), dma((2, 4, N_X)), dma((2, 4, N_X)),
            dma((2, 2, EXPERTS)), dma((2, 2, 2, EXPERTS)), dma((2, 2, EXPERTS)), dma((2, 2)),
            dma((2, 2, N_LO, 2)), dma((2, N_LO, 2)), dma((2, N_LO, N_C)), dma((2, 2, N_X, N_C)), dma((2, 2)),
            dma((2, N_HOST)), dma((2, N_HOST)),
        ],
        compiler_params=pltpu.CompilerParams(
            collective_id=0, has_side_effects=True, vmem_limit_bytes=VMEM_BYTES
        ),
        name="step",
    )(replica_plan, hid, grad_rows, master[0], moment_one[0], moment_two[0])
    weights_next, first_next, second_next = adam_update(master[0], moment_one[0], moment_two[0], gradient)
    return (weights_next[None], first_next[None], second_next[None], replica_weight[None])


def solution(mesh):
    return jax.shard_map(
        per_device,
        mesh=mesh,
        in_specs=(
            P(None, ("dp", "expert")),
            P(("dp", "expert"), None),
            P(("dp", "expert"), None),
            P(("dp", "expert")),
            P(),
            P("expert", "dp", None),
            P("expert", "dp", None),
            P("expert", "dp", None),
        ),
        out_specs=(
            P("expert", "dp", None),
            P("expert", "dp", None),
            P("expert", "dp", None),
            P("expert", "dp", None),
        ),
        check_vma=False,
    )
```
